128 devices in a mesh: scen: 32 (over x, z, core), pos: 4 (over y).
Axes of the slice: x: 4, y: 4, z: 4, core: 2. Of those that a mesh axis runs over, the one named last changes fastest.
Arguments:
- losses: bfloat16 [16384, 65536], P('scen', 'pos'), may hold values from -1 to 1
- book_sizes: int32 [1024], replicated, may hold values from 1 to 2048, 65536 in all
- owner_books: int32 [1024], replicated, may hold values from 0 to 1023, each once
Outputs:
- covariance: float32 [1024, 1024], P(('scen', 'pos'))
- contribution: float32 [1024], P(('scen', 'pos'))
The draws below stay inside these ranges and needn't reach their ends.
Inputs may be any that keep to these rules, and one draw needn't show every extreme that they name: `book_sizes`: book sizes are between 1 and 2048 and sum to 65536. `owner_books`: each book appears exactly once.
All inputs are finite; a program needn't handle non-finite values.
Results may differ from the reference program's by a relative error of at most 0.0003.
Values sent between devices are 32-bit elements; how exact they have to be, the bound alone decides.
A program may use at most 64 MiB of HBM per device.

```python
import math
import jax
import jax.numpy as jnp
import numpy as np
from jax import lax

POSITIONS = 65536
BOOKS = 1024
SCENARIOS = 16384


factor_count = 32


def draw_losses(key, part):
    loading_key = jax.random.fold_in(key, 101)
    loading = 0.02 * jax.random.normal(loading_key, (factor_count, POSITIONS), jnp.float32)
    height = math.gcd(SCENARIOS, 1024)

    def one_block(index):
        block_key = jax.random.fold_in(jax.random.fold_in(key, 107), index)
        factor_key = jax.random.fold_in(block_key, 1)
        noise_key = jax.random.fold_in(block_key, 2)
        factors = jax.random.normal(factor_key, (height, factor_count), jnp.float32)
        common = jnp.dot(factors, loading, precision=lax.Precision.HIGHEST, preferred_element_type=jnp.float32)
        specific = jax.random.uniform(noise_key, (height, POSITIONS), jnp.float32, -0.125, 0.375)
        return jnp.clip(specific + common, -1.0, 1.0).astype(jnp.bfloat16)
    blocks = lax.map(one_block, jnp.arange(SCENARIOS // height, dtype=jnp.int32))
    return blocks.reshape(SCENARIOS, POSITIONS)


def profile(number_of, total, bound, lean):
    loads = [(1 << 20) // math.isqrt(rank ** lean) + 1 for rank in range(2, number_of + 1)]
    surplus, counts = total - bound - (number_of - 1), [1] * (number_of - 1)
    while surplus > 0:
        movable = [i for i in range(number_of - 1) if counts[i] < bound]
        whole, remaining = sum([loads[i] for i in movable]), surplus
        for i in movable:
            extra = min(bound - counts[i], max(1, remaining * loads[i] // whole), surplus)
            counts[i] = counts[i] + extra
            surplus = surplus - extra
    return np.array([bound] + counts)


def ragged(rng, amount, total, bound, slope):
    if amount == 2:
        one = jax.random.randint(rng, (), max(1, total - bound), min(bound, total - 1) + 1)
        return jnp.stack([one, total - one])
    lengths = jnp.asarray(profile(amount, total, bound, slope), jnp.int32)
    twos = (amount - 1) // 2
    donor, receiver = lengths[1:1 + 2 * twos:2], lengths[2:2 + 2 * twos:2]
    room = jnp.minimum(donor - 1, bound - receiver)
    shifted = jax.random.randint(jax.random.fold_in(rng, 1), (twos,), 0, 1 << 20) % (room + 1)
    lengths = lengths.at[1:1 + 2 * twos:2].set(donor - shifted).at[2:2 + 2 * twos:2].set(receiver + shifted)
    return lengths[jax.random.permutation(jax.random.fold_in(rng, 2), amount)]


def setup_inputs(seed: int = 0) -> dict:
    key_of = jax.random.split(jax.random.key(seed), 4)
    losses = draw_losses(jax.random.fold_in(key_of[3], 71), 0)
    book_sizes = ragged(key_of[1], BOOKS, POSITIONS, POSITIONS // 32, 2).astype(jnp.int32)
    owner_books = jax.random.permutation(key_of[2], BOOKS).astype(jnp.int32)
    return dict(losses=losses, book_sizes=book_sizes, owner_books=owner_books)


def reference(losses, book_sizes, owner_books):
    start = jnp.cumsum(book_sizes) - book_sizes
    position = jnp.arange(POSITIONS, dtype=jnp.int32)
    book_of = (jnp.searchsorted(start, position, side='right') - 1).astype(jnp.int32)
    width = math.gcd(SCENARIOS, 1024)
    blocks = losses.reshape(SCENARIOS // width, width, POSITIONS)

    def block_sums(rows):
        summed = jax.ops.segment_sum(rows.astype(jnp.float32).T, book_of, num_segments=BOOKS)
        return summed.T
    book_pnl = lax.map(block_sums, blocks).reshape(SCENARIOS, BOOKS)
    book_mean = lax.optimization_barrier(jnp.sum(book_pnl, axis=0)) / SCENARIOS
    centered = book_pnl - book_mean
    reported = jnp.take(centered, owner_books, axis=1)
    covariance = jnp.dot(reported.T, centered, precision=lax.Precision.HIGHEST, preferred_element_type=jnp.float32) / SCENARIOS
    row_total = lax.optimization_barrier(jnp.sum(covariance, axis=1))
    portfolio_variance = jnp.sum(row_total)
    contribution = row_total / jnp.sqrt(portfolio_variance)
    return (covariance, contribution)
```

```python
import functools

import jax
import jax.numpy as jnp
from jax import lax
from jax.experimental import pallas as pl
from jax.experimental.pallas import tpu as pltpu
from jax.sharding import Mesh
from jax.sharding import PartitionSpec as P

LANES = 128
TILE = 256
BLOCK = 4096
SHORT = 384
X, Z, C, Y = "scen_0", "scen_1", "scen_2", "pos"
SCEN = (X, Z, C)
SCEN_POS = (X, Z, C, Y)
COLOURS = (((X, 0), (Z, 0), (Y, 0)), ((Z, 1), (Y, 1), (X, 0)), ((Y, 2), (X, 0), (Z, 0)))


def segsum_body(lo_ref, hi_ref, start_ref, x_ref, out_ref, col):
    step = pl.program_id(0)
    width = x_ref.shape[1]

    @pl.when(step == 0)
    def _():
        out_ref[...] = jnp.zeros_like(out_ref)
        for b in range(0, col.shape[0], LANES):
            row = start_ref[:, b : b + LANES]
            col[b : b + LANES, :] = jnp.broadcast_to(row, (LANES, LANES)).T

    base = step * width
    lane = lax.broadcasted_iota(jnp.int32, (TILE, LANES), 1)

    def add_tile(t, carry):
        r0 = pl.multiple_of(t * TILE, TILE)
        begin = col[pl.ds(r0, TILE), :] - base
        end = col[pl.ds(r0 + 1, TILE), :] - base
        parts = []
        for l in range(0, width, LANES):
            place = lane + l
            inside = (place >= begin) & (place < end)
            parts.append(jnp.where(inside, 1.0, 0.0).astype(jnp.bfloat16))
        member = jnp.concatenate(parts, axis=1)
        sums = lax.dot_general(
            member, x_ref[...], (((1,), (1,)), ((), ())), preferred_element_type=jnp.float32
        )
        for c in range(out_ref.shape[0]):
            out_ref[c, pl.ds(r0, TILE), :] += sums[:, LANES * c : LANES * (c + 1)]
        return carry

    lax.fori_loop(lo_ref[step], hi_ref[step] + 1, add_tile, 0)


def segment_sums(losses, start, lo, hi, books):
    rows, places = losses.shape
    whole = lambda i, *_: (0, 0)
    return pl.pallas_call(
        segsum_body,
        out_shape=jax.ShapeDtypeStruct((rows // LANES, books, LANES), jnp.float32),
        grid_spec=pltpu.PrefetchScalarGridSpec(
            num_scalar_prefetch=2,
            grid=(places // BLOCK,),
            in_specs=[
                pl.BlockSpec(start.shape, whole),
                pl.BlockSpec((rows, BLOCK), lambda i, *_: (0, i)),
            ],
            out_specs=pl.BlockSpec((rows // LANES, books, LANES), lambda i, *_: (0, 0, 0)),
            scratch_shapes=[pltpu.VMEM((start.shape[1], LANES), jnp.int32)],
        ),
        name="segment_sums",
        compiler_params=pltpu.CompilerParams(
            dimension_semantics=("arbitrary",), vmem_limit_bytes=40 << 20
        ),
    )(lo, hi, start, losses)


def split(x):
    high = x.astype(jnp.bfloat16)
    return high, (x - high.astype(jnp.float32)).astype(jnp.bfloat16)


def to_column(row):
    return jnp.broadcast_to(row, (LANES, LANES)).T


def exchange_body(
    cap, total, offs, owner, xc, cov, con,
    land, vsum, vland, yvec, z, full0, full1, own, gram, land1, land2, land3, part1, part2,
    ysend, yrecv, vsend, vrecv, psend, precv, rsend, rrecv,
):
    at = {name: lax.axis_index(name) for name in SCEN_POS}
    size = {X: 4, Z: 4, C: 2, Y: 4}
    full = (full0, full1)
    books = full0.shape[0]

    def peer(name, p):
        return lax.rem(at[name] + p, size[name])

    barrier = pltpu.get_barrier_semaphore()
    count = 0
    for name in SCEN_POS:
        for p in range(1, size[name]):
            pl.semaphore_signal(
                barrier, inc=1, device_id={name: peer(name, p)}, device_id_type=pl.DeviceIdType.MESH
            )
            count += 1
    pl.semaphore_wait(barrier, count)

    def send(src, dst, s, r, name, p):
        copy = pltpu.make_async_remote_copy(
            src_ref=src,
            dst_ref=dst,
            send_sem=s,
            recv_sem=r,
            device_id={name: peer(name, p)},
            device_id_type=pl.DeviceIdType.MESH,
        )
        copy.start()
        return copy

    started = []
    chunks = []
    for p in (2, 1, 3):
        chunks.append(
            send(
                xc.at[peer(Y, p), pl.ds(0, cap), :], land.at[p - 1],
                ysend.at[p - 1], yrecv.at[p - 1], Y, p,
            )
        )

    for b in range(0, cap, LANES):
        rows = slice(b, b + LANES)
        block = (xc[0, rows, :] + xc[1, rows, :]) + (xc[2, rows, :] + xc[3, rows, :])
        vsum[0, :, rows] = block.T.reshape(LANES // 8, 8, LANES).sum(axis=0)
    slot = 0
    for stage, name in enumerate((X, Z, C)):
        copies = []
        for p in range(1, size[name]):
            copies.append(
                send(vsum.at[stage], vland.at[slot], vsend.at[slot], vrecv.at[slot], name, p)
            )
            slot += 1
        value = vsum[stage]
        for n, copy in enumerate(copies):
            copy.wait_recv()
            value = value + vland[slot - len(copies) + n]
        vsum[stage + 1] = value
        started += copies
    ycopies = []
    for p in range(1, 4):
        ycopies.append(send(vsum.at[3], yvec.at[p - 1], vsend.at[slot], vrecv.at[slot], Y, p))
        slot += 1
    started += ycopies

    zero = jnp.zeros((8, LANES), jnp.float32)

    def centre(p, values, sums):
        z[p, 0:8, :] = zero
        z[p, cap + 8 : cap + 16, :] = zero
        mean = sums.sum(axis=0, keepdims=True) / total
        for b in range(0, cap, LANES):
            z[p, 8 + b : 8 + b + LANES, :] = values[b : b + LANES, :] - to_column(
                mean[:, b : b + LANES]
            )

    centre(0, xc.at[at[Y]], vsum[3])
    for n, p in enumerate((2, 1, 3)):
        ycopies[p - 1].wait_recv()
        chunks[n].wait_recv()
        centre(p, land.at[p - 1], yvec[p - 1])
    started += chunks

    first = [offs[lax.rem(at[Y] + 4 - p, 4)] for p in range(4)]

    def put(t, carry):
        row = t * 8
        value = None
        for p in range(4):
            u = lax.min(lax.max(row - first[p] + 8, 0), cap + 8)
            got = z[p, pl.ds(u, 8), :]
            value = got if value is None else value + got
        full0[pl.ds(pl.multiple_of(row, 8), 8), :] = value
        return carry

    lax.fori_loop(0, books // 8, put, 0, unroll=8)
    pair = send(full0, full1, psend, precv, C, 1)
    started.append(pair)

    core = at[C]

    def gather(h):
        def some(g, carry):
            k0 = (g // 4) * 64 + core * 32 + lax.rem(g, 4) * 8
            for r in range(8):
                book = owner[k0 + r]
                own[h, pl.ds(g * 8 + r, 1), :] = full[h][pl.ds(book, 1), :]
            return carry

        lax.fori_loop(0, own.shape[1] // 8, some, 0, unroll=2)

    gather(0)
    pair.wait_recv()
    gather(1)

    sums = [full[h][...].reshape(books // 8, 8, LANES).sum(axis=0).sum(axis=0, keepdims=True) for h in (0, 1)]
    square = (sums[0] * sums[0] + sums[1] * sums[1]).sum(axis=1, keepdims=True)
    gram[:, :, :, :, books : books + LANES] = jnp.broadcast_to(square, (4, 4, 4, 8, LANES))

    a0h, a0l = split(own[0])
    a1h, a1l = split(own[1])
    left = jnp.concatenate([a0h, a1h, a0h, a1h, a0l, a1l], axis=1)
    for b in range(0, books, TILE):
        b0h, b0l = split(full0[b : b + TILE, :])
        b1h, b1l = split(full1[b : b + TILE, :])
        right = jnp.concatenate([b0h, b1h, b0l, b1l, b0h, b1h], axis=1)
        got = lax.dot_general(
            left, right, (((1,), (1,)), ((), ())), preferred_element_type=jnp.float32
        )
        gram[:, :, :, :, b : b + TILE] = got.reshape(4, 4, 4, 8, TILE)

    third = gram.shape[4] // 3

    def pick(ref, dim, index):
        return ref.at[(slice(None),) * dim + (index,)]

    def scatter(stage, colour, source, lands):
        name, dim = COLOURS[colour][stage]
        copies = []
        for p in (2, 1, 3):
            copies.append(
                (p, send(
                    pick(source, dim, peer(name, p)), lands.at[colour, p - 1],
                    rsend.at[stage, colour, p - 1], rrecv.at[stage, colour, p - 1], name, p,
                ))
            )
        return copies

    def reduce(stage, colour, source, lands, copies):
        name, dim = COLOURS[colour][stage]
        value = pick(source, dim, at[name])[...]
        for p, copy in copies:
            copy.wait_recv()
            value = value + lands[colour, p - 1]
            started.append(copy)
        return value

    sources = [gram.at[:, :, :, :, pl.ds(third * c, third)] for c in range(3)]
    flying = [scatter(0, c, sources[c], land1) for c in range(3)]
    for c in range(3):
        part1[c] = reduce(0, c, sources[c], land1, flying[c])
        flying[c] = scatter(1, c, part1.at[c], land2)
    for c in range(3):
        part2[c] = reduce(1, c, part1.at[c], land2, flying[c])
        flying[c] = scatter(2, c, part2.at[c], land3)
    done = [reduce(2, c, part2.at[c], land3, flying[c]) for c in range(3)]
    last = books - 2 * third
    cov[:, 0:third] = done[0] / total
    cov[:, third : 2 * third] = done[1] / total
    cov[:, 2 * third :] = done[2][:, :last] / total
    row = cov[...].sum(axis=1, keepdims=True)
    variance = done[2][:, last : last + 1] / total
    con[...] = jnp.broadcast_to(row / jnp.sqrt(variance), con.shape)
    for copy in started:
        copy.wait_send()


def exchange(xc, first, owner, cap, total, collective):
    books = xc.shape[1]
    f32 = jnp.float32
    third = (books + LANES) // 3
    rows = books // 128
    dma = pltpu.SemaphoreType.DMA
    return pl.pallas_call(
        functools.partial(exchange_body, cap, total),
        out_shape=(
            jax.ShapeDtypeStruct((rows, books), f32),
            jax.ShapeDtypeStruct((rows, LANES), f32),
        ),
        in_specs=[
            pl.BlockSpec(memory_space=pltpu.SMEM),
            pl.BlockSpec(memory_space=pltpu.SMEM),
            pl.BlockSpec(memory_space=pltpu.VMEM),
        ],
        out_specs=[pl.BlockSpec(memory_space=pltpu.VMEM)] * 2,
        scratch_shapes=[
            pltpu.VMEM((3, cap, LANES), f32),
            pltpu.VMEM((4, 8, cap), f32),
            pltpu.VMEM((7, 8, cap), f32),
            pltpu.VMEM((3, 8, cap), f32),
            pltpu.VMEM((4, cap + 16, LANES), f32),
            pltpu.VMEM((books, LANES), f32),
            pltpu.VMEM((books, LANES), f32),
            pltpu.VMEM((2, books // 2, LANES), f32),
            pltpu.VMEM((4, 4, 4, 8, books + LANES), f32),
            pltpu.VMEM((3, 3, 4, 4, 8, third), f32),
            pltpu.VMEM((3, 3, 4, 8, third), f32),
            pltpu.VMEM((3, 3, 8, third), f32),
            pltpu.VMEM((3, 4, 4, 8, third), f32),
            pltpu.VMEM((3, 4, 8, third), f32),
            dma((3,)), dma((3,)), dma((10,)), dma((10,)), dma, dma,
            dma((3, 3, 3)), dma((3, 3, 3)),
        ],
        name="exchange_%d" % cap,
        compiler_params=pltpu.CompilerParams(
            collective_id=collective, has_side_effects=True, vmem_limit_bytes=40 << 20
        ),
    )(first, owner, xc)


def per_device(losses, book_sizes, owner_books):
    rows, places = losses.shape
    books = book_sizes.shape[0]
    me = lax.axis_index(Y)
    total = rows * lax.axis_size(SCEN)
    finish = jnp.cumsum(book_sizes)

    def book_at(place):
        return jnp.sum((finish[None, :] <= place[:, None]).astype(jnp.int32), axis=1)

    blocks = jnp.arange(4, dtype=jnp.int32) * places
    first = book_at(blocks) // 8 * 8
    mine = jnp.take(first, me)
    beyond = jnp.full((books + LANES,), 1 << 24, jnp.int32)
    starts = jnp.concatenate([finish - book_sizes, beyond])
    start = lax.dynamic_slice(starts, (mine,), (books + LANES,)) - me * places
    ahead = me * places + BLOCK * jnp.arange(places // BLOCK, dtype=jnp.int32)
    lo = (book_at(ahead) - mine) // TILE
    hi = (book_at(ahead + (BLOCK - 1)) - mine) // TILE
    xc = segment_sums(losses, start.reshape(1, -1), lo, hi, books)
    cov, con = exchange(xc, first, owner_books, books, total, 1)
    return cov, con[:, 0]


def solution(mesh):
    grid = Mesh(mesh.devices.reshape(4, 4, 2, mesh.shape["pos"]), SCEN_POS)
    return jax.shard_map(
        per_device,
        mesh=grid,
        in_specs=(P(SCEN, Y), P(), P()),
        out_specs=(P(SCEN_POS, None), P(SCEN_POS)),
        check_vma=False,
    )
```

```python
import functools

import jax
import jax.numpy as jnp
from jax import lax
from jax.experimental import pallas as pl
from jax.experimental.pallas import tpu as pltpu
from jax.sharding import Mesh
from jax.sharding import PartitionSpec as P

LANES = 128
TILE = 256
BLOCK = 4096
SHORT = 384
X, Z, C, Y = "scen_0", "scen_1", "scen_2", "pos"
SCEN = (X, Z, C)
SCEN_POS = (X, Z, C, Y)
COLOURS = (((X, 0), (Z, 0), (Y, 0)), ((Z, 1), (Y, 1), (X, 0)), ((Y, 2), (X, 0), (Z, 0)))


def segsum_body(lo_ref, hi_ref, start_ref, x_ref, out_ref, col):
    step = pl.program_id(0)
    width = x_ref.shape[1]

    @pl.when(step == 0)
    def _():
        out_ref[...] = jnp.zeros_like(out_ref)
        for b in range(0, col.shape[0], LANES):
            row = start_ref[:, b : b + LANES]
            col[b : b + LANES, :] = jnp.broadcast_to(row, (LANES, LANES)).T

    base = step * width
    lane = lax.broadcasted_iota(jnp.int32, (TILE, LANES), 1)

    def add_tile(t, carry):
        r0 = pl.multiple_of(t * TILE, TILE)
        begin = col[pl.ds(r0, TILE), :] - base
        end = col[pl.ds(r0 + 1, TILE), :] - base
        parts = []
        for l in range(0, width, LANES):
            place = lane + l
            inside = (place >= begin) & (place < end)
            parts.append(jnp.where(inside, 1.0, 0.0).astype(jnp.bfloat16))
        member = jnp.concatenate(parts, axis=1)
        sums = lax.dot_general(
            member, x_ref[...], (((1,), (1,)), ((), ())), preferred_element_type=jnp.float32
        )
        for c in range(out_ref.shape[0]):
            out_ref[c, pl.ds(r0, TILE), :] += sums[:, LANES * c : LANES * (c + 1)]
        return carry

    lax.fori_loop(lo_ref[step], hi_ref[step] + 1, add_tile, 0)


def segment_sums(losses, start, lo, hi, books):
    rows, places = losses.shape
    whole = lambda i, *_: (0, 0)
    return pl.pallas_call(
        segsum_body,
        out_shape=jax.ShapeDtypeStruct((rows // LANES, books, LANES), jnp.float32),
        grid_spec=pltpu.PrefetchScalarGridSpec(
            num_scalar_prefetch=2,
            grid=(places // BLOCK,),
            in_specs=[
                pl.BlockSpec(start.shape, whole),
                pl.BlockSpec((rows, BLOCK), lambda i, *_: (0, i)),
            ],
            out_specs=pl.BlockSpec((rows // LANES, books, LANES), lambda i, *_: (0, 0, 0)),
            scratch_shapes=[pltpu.VMEM((start.shape[1], LANES), jnp.int32)],
        ),
        name="segment_sums",
        compiler_params=pltpu.CompilerParams(
            dimension_semantics=("arbitrary",), vmem_limit_bytes=40 << 20
        ),
    )(lo, hi, start, losses)


def split(x):
    high = x.astype(jnp.bfloat16)
    return high, (x - high.astype(jnp.float32)).astype(jnp.bfloat16)


def to_column(row):
    return jnp.broadcast_to(row, (LANES, LANES)).T


def exchange_body(
    cap, total, offs, owners, xc, cov, con,
    owner, land, vsum, vland, yvec, z, full0, full1, own, gram, land1, land2, land3, part1, part2,
    ysend, yrecv, vsend, vrecv, psend, precv, rsend, rrecv, osem,
):
    at = {name: lax.axis_index(name) for name in SCEN_POS}
    size = {X: 4, Z: 4, C: 2, Y: 4}
    full = (full0, full1)
    books = full0.shape[0]

    def peer(name, p):
        return lax.rem(at[name] + p, size[name])

    fetch = pltpu.make_async_copy(owners, owner, osem)
    fetch.start()
    others = [{name: peer(name, p)} for name in SCEN_POS for p in range(1, size[name])]
    others += [{C: peer(C, 1), Y: peer(Y, p)} for p in range(1, size[Y])]
    barrier = pltpu.get_barrier_semaphore()
    for other in others:
        pl.semaphore_signal(barrier, inc=1, device_id=other, device_id_type=pl.DeviceIdType.MESH)
    pl.semaphore_wait(barrier, len(others))

    def send_to(src, dst, s, r, device):
        copy = pltpu.make_async_remote_copy(
            src_ref=src,
            dst_ref=dst,
            send_sem=s,
            recv_sem=r,
            device_id=device,
            device_id_type=pl.DeviceIdType.MESH,
        )
        copy.start()
        return copy

    def send(src, dst, s, r, name, p):
        return send_to(src, dst, s, r, {name: peer(name, p)})

    started = []
    chunks = []
    for p in (2, 1, 3):
        chunks.append(
            send(
                xc.at[peer(Y, p), pl.ds(0, cap), :], land.at[p - 1],
                ysend.at[p - 1], yrecv.at[p - 1], Y, p,
            )
        )

    for b in range(0, cap, LANES):
        rows = slice(b, b + LANES)
        block = (xc[0, rows, :] + xc[1, rows, :]) + (xc[2, rows, :] + xc[3, rows, :])
        vsum[0, :, rows] = block.T.reshape(LANES // 8, 8, LANES).sum(axis=0)
    slot = 0
    for stage, name in enumerate((X, Z)):
        copies = []
        for p in range(1, size[name]):
            copies.append(
                send(vsum.at[stage], vland.at[slot], vsend.at[slot], vrecv.at[slot], name, p)
            )
            slot += 1
        value = vsum[stage]
        for n, copy in enumerate(copies):
            copy.wait_recv()
            value = value + vland[slot - len(copies) + n]
        vsum[stage + 1] = value
        started += copies
    ycopies = {}
    for p in (2, 1, 3, 0):
        for d in (0, 1):
            if p or d:
                ycopies[d, p] = send_to(
                    vsum.at[2], yvec.at[4 * d + p], vsend.at[slot], vrecv.at[slot],
                    {C: peer(C, d), Y: peer(Y, p)},
                )
                slot += 1
    started += ycopies.values()

    zero = jnp.zeros((8, LANES), jnp.float32)

    def centre(p, values, sums):
        z[p, 0:8, :] = zero
        z[p, cap + 8 : cap + 16, :] = zero
        mean = sums.sum(axis=0, keepdims=True) / total
        for b in range(0, cap, LANES):
            z[p, 8 + b : 8 + b + LANES, :] = values[b : b + LANES, :] - to_column(
                mean[:, b : b + LANES]
            )

    ycopies[1, 0].wait_recv()
    centre(0, xc.at[at[Y]], vsum[2] + yvec[4])
    for n, p in ((1, 1), (2, 3), (0, 2)):
        ycopies[0, p].wait_recv()
        ycopies[1, p].wait_recv()
        chunks[n].wait_recv()
        centre(p, land.at[p - 1], yvec[p] + yvec[4 + p])
    started += chunks

    first = [offs[lax.rem(at[Y] + 4 - p, 4)] for p in range(4)]

    def put(t, carry):
        row = t * 8
        value = None
        for p in range(4):
            u = lax.min(lax.max(row - first[p] + 8, 0), cap + 8)
            got = z[p, pl.ds(u, 8), :]
            value = got if value is None else value + got
        full0[pl.ds(pl.multiple_of(row, 8), 8), :] = value
        return carry

    lax.fori_loop(0, books // 8, put, 0, unroll=8)
    pair = send(full0, full1, psend, precv, C, 1)
    started.append(pair)

    core = at[C]

    def gather(h):
        def some(g, carry):
            k0 = (g // 4) * 64 + core * 32 + lax.rem(g, 4) * 8
            for r in range(8):
                book = owner[k0 + r]
                own[h, pl.ds(g * 8 + r, 1), :] = full[h][pl.ds(book, 1), :]
            return carry

        lax.fori_loop(0, own.shape[1] // 8, some, 0, unroll=2)

    fetch.wait()
    gather(0)
    pair.wait_recv()
    gather(1)

    sums = [full[h][...].reshape(books // 8, 8, LANES).sum(axis=0).sum(axis=0, keepdims=True) for h in (0, 1)]
    square = (sums[0] * sums[0] + sums[1] * sums[1]).sum(axis=1, keepdims=True)
    gram[:, :, :, :, books : books + LANES] = jnp.broadcast_to(square, (4, 4, 4, 8, LANES))

    a0h, a0l = split(own[0])
    a1h, a1l = split(own[1])
    left = jnp.concatenate([a0h, a1h, a0h, a1h, a0l, a1l], axis=1)
    for b in range(0, books, TILE):
        b0h, b0l = split(full0[b : b + TILE, :])
        b1h, b1l = split(full1[b : b + TILE, :])
        right = jnp.concatenate([b0h, b1h, b0l, b1l, b0h, b1h], axis=1)
        got = lax.dot_general(
            left, right, (((1,), (1,)), ((), ())), preferred_element_type=jnp.float32
        )
        gram[:, :, :, :, b : b + TILE] = got.reshape(4, 4, 4, 8, TILE)

    third = gram.shape[4] // 3

    def pick(ref, dim, index):
        return ref.at[(slice(None),) * dim + (index,)]

    def scatter(stage, colour, source, lands):
        name, dim = COLOURS[colour][stage]
        copies = []
        for p in (2, 1, 3):
            copies.append(
                (p, send(
                    pick(source, dim, peer(name, p)), lands.at[colour, p - 1],
                    rsend.at[stage, colour, p - 1], rrecv.at[stage, colour, p - 1], name, p,
                ))
            )
        return copies

    def reduce(stage, colour, source, lands, copies):
        name, dim = COLOURS[colour][stage]
        value = pick(source, dim, at[name])[...]
        for p, copy in copies:
            copy.wait_recv()
            value = value + lands[colour, p - 1]
            started.append(copy)
        return value

    sources = [gram.at[:, :, :, :, pl.ds(third * c, third)] for c in range(3)]
    flying = [scatter(0, c, sources[c], land1) for c in range(3)]
    for c in range(3):
        part1[c] = reduce(0, c, sources[c], land1, flying[c])
        flying[c] = scatter(1, c, part1.at[c], land2)
    for c in range(3):
        part2[c] = reduce(1, c, part1.at[c], land2, flying[c])
        flying[c] = scatter(2, c, part2.at[c], land3)
    done = [reduce(2, c, part2.at[c], land3, flying[c]) for c in range(3)]
    last = books - 2 * third
    cov[:, 0:third] = done[0] / total
    cov[:, third : 2 * third] = done[1] / total
    cov[:, 2 * third :] = done[2][:, :last] / total
    row = cov[...].sum(axis=1, keepdims=True)
    variance = done[2][:, last : last + 1] / total
    con[...] = jnp.broadcast_to(row / jnp.sqrt(variance), con.shape)
    for copy in started:
        copy.wait_send()


def exchange(xc, first, owner, cap, total, collective):
    books = xc.shape[1]
    f32 = jnp.float32
    third = (books + LANES) // 3
    rows = books // 128
    dma = pltpu.SemaphoreType.DMA
    return pl.pallas_call(
        functools.partial(exchange_body, cap, total),
        out_shape=(
            jax.ShapeDtypeStruct((rows, books), f32),
            jax.ShapeDtypeStruct((rows, LANES), f32),
        ),
        in_specs=[
            pl.BlockSpec(memory_space=pltpu.SMEM),
            pl.BlockSpec(memory_space=pl.ANY),
            pl.BlockSpec(memory_space=pltpu.VMEM),
        ],
        out_specs=[pl.BlockSpec(memory_space=pltpu.VMEM)] * 2,
        scratch_shapes=[
            pltpu.SMEM(owner.shape, jnp.int32),
            pltpu.VMEM((3, cap, LANES), f32),
            pltpu.VMEM((3, 8, cap), f32),
            pltpu.VMEM((6, 8, cap), f32),
            pltpu.VMEM((8, 8, cap), f32),
            pltpu.VMEM((4, cap + 16, LANES), f32),
            pltpu.VMEM((books, LANES), f32),
            pltpu.VMEM((books, LANES), f32),
            pltpu.VMEM((2, books // 2, LANES), f32),
            pltpu.VMEM((4, 4, 4, 8, books + LANES), f32),
            pltpu.VMEM((3, 3, 4, 4, 8, third), f32),
            pltpu.VMEM((3, 3, 4, 8, third), f32),
            pltpu.VMEM((3, 3, 8, third), f32),
            pltpu.VMEM((3, 4, 4, 8, third), f32),
            pltpu.VMEM((3, 4, 8, third), f32),
            dma((3,)), dma((3,)), dma((13,)), dma((13,)), dma, dma,
            dma((3, 3, 3)), dma((3, 3, 3)), dma,
        ],
        name="exchange_%d" % cap,
        compiler_params=pltpu.CompilerParams(
            collective_id=collective, has_side_effects=True, vmem_limit_bytes=40 << 20
        ),
    )(first, owner, xc)


def per_device(losses, book_sizes, owner_books):
    rows, places = losses.shape
    books = book_sizes.shape[0]
    me = lax.axis_index(Y)
    total = rows * lax.axis_size(SCEN)
    finish = jnp.cumsum(book_sizes)

    def book_at(place):
        return jnp.sum((finish[None, :] <= place[:, None]).astype(jnp.int32), axis=1)

    blocks = jnp.arange(4, dtype=jnp.int32) * places
    first = book_at(blocks) // 8 * 8
    mine = jnp.take(first, me)
    beyond = jnp.full((books + LANES,), 1 << 24, jnp.int32)
    starts = jnp.concatenate([finish - book_sizes, beyond])
    start = lax.dynamic_slice(starts, (mine,), (books + LANES,)) - me * places
    ahead = me * places + BLOCK * jnp.arange(places // BLOCK, dtype=jnp.int32)
    lo = (book_at(ahead) - mine) // TILE
    hi = (book_at(ahead + (BLOCK - 1)) - mine) // TILE
    xc = segment_sums(losses, start.reshape(1, -1), lo, hi, books)
    last = book_at(blocks + (places - 1))
    fits = jnp.max(last - first) < SHORT
    cov, con = lax.cond(
        fits,
        lambda *a: exchange(*a, SHORT, total, 1),
        lambda *a: exchange(*a, books, total, 2),
        xc, first, owner_books,
    )
    return cov, con[:, 0]


def solution(mesh):
    grid = Mesh(mesh.devices.reshape(4, 4, 2, mesh.shape["pos"]), SCEN_POS)
    return jax.shard_map(
        per_device,
        mesh=grid,
        in_specs=(P(SCEN, Y), P(), P()),
        out_specs=(P(SCEN_POS, None), P(SCEN_POS)),
        check_vma=False,
    )
```

```python
import functools

import jax
import jax.numpy as jnp
from jax import lax
from jax.experimental import pallas as pl
from jax.experimental.pallas import tpu as pltpu
from jax.sharding import Mesh
from jax.sharding import PartitionSpec as P

LANES = 128
TILE = 256
SHORT = 384
X, Z, C, Y = "scen_0", "scen_1", "scen_2", "pos"
SCEN = (X, Z, C)
SCEN_POS = (X, Z, C, Y)
COLOURS = (((X, 0), (Z, 0), (Y, 0)), ((Z, 1), (Y, 1), (X, 0)), ((Y, 2), (X, 0), (Z, 0)))


def segsum_body(blocks, sizes_ref, x_hbm, out_ref, facts_ref, kept, col, sems):
    books = out_ref.shape[1]
    places = x_hbm.shape[1]
    me = lax.axis_index(Y)
    f32 = jnp.float32
    copies = []
    for n, (at, width) in enumerate(blocks):
        piece = pl.ds(at, width)
        copies.append(pltpu.make_async_copy(x_hbm.at[:, piece], kept.at[:, piece], sems.at[n]))
        copies[-1].start()

    exact = lax.Precision.HIGHEST
    sizes = sizes_ref[...].astype(f32)
    down = lax.broadcasted_iota(jnp.int32, (LANES, LANES), 0)
    across = lax.broadcasted_iota(jnp.int32, (LANES, LANES), 1)
    upper = jnp.where(down <= across, 1.0, 0.0).astype(f32)
    within = jnp.dot(sizes, upper, precision=exact, preferred_element_type=f32)
    before = [jnp.zeros((1, LANES), f32)]
    for k in range(books // LANES - 1):
        before.append(before[-1] + within[k : k + 1, LANES - 1 : LANES])
    start = within - sizes + jnp.concatenate(before, axis=0)
    for k in range(books // LANES):
        col[LANES * k : LANES * (k + 1), :] = to_column(start[k : k + 1, :]).astype(jnp.int32)
    col[books:, :] = jnp.full((col.shape[0] - books, LANES), 1 << 24, jnp.int32)

    lane = lax.broadcasted_iota(jnp.int32, (1, LANES), 1)
    place = jnp.zeros((1, LANES), jnp.int32)
    for n, (at, width) in enumerate(blocks):
        place = jnp.where(lane == n, me * places + at, place)
        place = jnp.where(lane == 16 + n, me * places + at + width - 1, place)
    for j in range(4):
        place = jnp.where(lane == 32 + j, j * places, place)
        place = jnp.where(lane == 48 + j, j * places + places - 1, place)
    count = jnp.zeros((8, LANES), jnp.int32)
    for b in range(0, books, 8):
        count = count + jnp.where(col[b : b + 8, :] <= place, 1, 0)
    facts = jnp.sum(count, axis=0, keepdims=True) - 1
    facts = jnp.where((lane >= 32) & (lane < 48), facts // 8 * 8, facts)

    def fact(i):
        return jnp.sum(jnp.where(lane == i, facts, 0).astype(f32)).astype(jnp.int32)

    longest = fact(48) - fact(32)
    for j in range(1, 4):
        longest = jnp.maximum(longest, fact(48 + j) - fact(32 + j))
    facts_ref[...] = jnp.where(lane == 64, longest, facts)
    mine = fact(32 + me)
    spans = [((fact(n) - mine) // TILE, (fact(16 + n) - mine) // TILE) for n in range(len(blocks))]
    out_ref[...] = jnp.zeros_like(out_ref)

    lanes = lax.broadcasted_iota(jnp.int32, (TILE, LANES), 1)
    for n, (at, width) in enumerate(blocks):
        base = me * places + at
        copies[n].wait()

        def add_tile(t, carry):
            r0 = pl.multiple_of(t * TILE, TILE)
            g0 = pl.multiple_of(mine + r0, 8)
            begin = col[pl.ds(g0, TILE), :] - base
            end = col[pl.ds(g0 + 1, TILE), :] - base
            parts = []
            for l in range(0, width, LANES):
                inside = (lanes + l >= begin) & (lanes + l < end)
                parts.append(jnp.where(inside, 1.0, 0.0).astype(jnp.bfloat16))
            sums = lax.dot_general(
                jnp.concatenate(parts, axis=1), kept[:, at : at + width],
                (((1,), (1,)), ((), ())), preferred_element_type=f32,
            )
            for c in range(out_ref.shape[0]):
                out_ref[c, pl.ds(r0, TILE), :] += sums[:, LANES * c : LANES * (c + 1)]
            return carry

        lax.fori_loop(spans[n][0], spans[n][1] + 1, add_tile, 0)


def segment_sums(losses, sizes):
    rows, places = losses.shape
    books = sizes.shape[0]
    widths = [places // 4] * 3 + [places // 8] * 2
    blocks = tuple((sum(widths[:n]), w) for n, w in enumerate(widths))
    return pl.pallas_call(
        functools.partial(segsum_body, blocks),
        out_shape=(
            jax.ShapeDtypeStruct((rows // LANES, books, LANES), jnp.float32),
            jax.ShapeDtypeStruct((1, LANES), jnp.int32),
        ),
        in_specs=[pl.BlockSpec(memory_space=pltpu.VMEM), pl.BlockSpec(memory_space=pl.ANY)],
        out_specs=[pl.BlockSpec(memory_space=pltpu.VMEM)] * 2,
        scratch_shapes=[
            pltpu.VMEM((rows, places), jnp.bfloat16),
            pltpu.VMEM((2 * books + TILE, LANES), jnp.int32),
            pltpu.SemaphoreType.DMA((len(blocks),)),
        ],
        name="segment_sums",
        compiler_params=pltpu.CompilerParams(vmem_limit_bytes=48 << 20),
    )(sizes.reshape(books // LANES, LANES), losses)


def split(x):
    high = x.astype(jnp.bfloat16)
    return high, (x - high.astype(jnp.float32)).astype(jnp.bfloat16)


def to_column(row):
    return jnp.broadcast_to(row, (LANES, LANES)).T


def exchange_body(
    cap, total, offs, owners, xc, cov, con,
    owner, land, vsum, vland, yvec, z, full0, full1, own, gram, land1, land2, land3, part1, part2,
    ysend, yrecv, vsend, vrecv, psend, precv, rsend, rrecv, osem,
):
    at = {name: lax.axis_index(name) for name in SCEN_POS}
    size = {X: 4, Z: 4, C: 2, Y: 4}
    full = (full0, full1)
    books = full0.shape[0]

    def peer(name, p):
        return lax.rem(at[name] + p, size[name])

    fetch = pltpu.make_async_copy(owners, owner, osem)
    fetch.start()
    others = [{name: peer(name, p)} for name in SCEN_POS for p in range(1, size[name])]
    others += [{C: peer(C, 1), Y: peer(Y, p)} for p in range(1, size[Y])]
    barrier = pltpu.get_barrier_semaphore()
    for other in others:
        pl.semaphore_signal(barrier, inc=1, device_id=other, device_id_type=pl.DeviceIdType.MESH)
    pl.semaphore_wait(barrier, len(others))

    def send_to(src, dst, s, r, device):
        copy = pltpu.make_async_remote_copy(
            src_ref=src,
            dst_ref=dst,
            send_sem=s,
            recv_sem=r,
            device_id=device,
            device_id_type=pl.DeviceIdType.MESH,
        )
        copy.start()
        return copy

    def send(src, dst, s, r, name, p):
        return send_to(src, dst, s, r, {name: peer(name, p)})

    started = []
    chunks = []
    for p in (2, 1, 3):
        chunks.append(
            send(
                xc.at[peer(Y, p), pl.ds(0, cap), :], land.at[p - 1],
                ysend.at[p - 1], yrecv.at[p - 1], Y, p,
            )
        )

    for b in range(0, cap, LANES):
        rows = slice(b, b + LANES)
        block = (xc[0, rows, :] + xc[1, rows, :]) + (xc[2, rows, :] + xc[3, rows, :])
        vsum[0, :, rows] = block.T.reshape(LANES // 8, 8, LANES).sum(axis=0)
    slot = 0
    for stage, name in enumerate((X, Z)):
        copies = []
        for p in range(1, size[name]):
            copies.append(
                send(vsum.at[stage], vland.at[slot], vsend.at[slot], vrecv.at[slot], name, p)
            )
            slot += 1
        value = vsum[stage]
        for n, copy in enumerate(copies):
            copy.wait_recv()
            value = value + vland[slot - len(copies) + n]
        vsum[stage + 1] = value
        started += copies
    ycopies = {}
    for p in (2, 1, 3, 0):
        for d in (0, 1):
            if p or d:
                ycopies[d, p] = send_to(
                    vsum.at[2], yvec.at[4 * d + p], vsend.at[slot], vrecv.at[slot],
                    {C: peer(C, d), Y: peer(Y, p)},
                )
                slot += 1
    started += ycopies.values()

    zero = jnp.zeros((8, LANES), jnp.float32)

    def centre(p, values, sums):
        z[p, 0:8, :] = zero
        z[p, cap + 8 : cap + 16, :] = zero
        mean = sums.sum(axis=0, keepdims=True) / total
        for b in range(0, cap, LANES):
            z[p, 8 + b : 8 + b + LANES, :] = values[b : b + LANES, :] - to_column(
                mean[:, b : b + LANES]
            )

    ycopies[1, 0].wait_recv()
    centre(0, xc.at[at[Y]], vsum[2] + yvec[4])
    for n, p in ((1, 1), (2, 3), (0, 2)):
        ycopies[0, p].wait_recv()
        ycopies[1, p].wait_recv()
        chunks[n].wait_recv()
        centre(p, land.at[p - 1], yvec[p] + yvec[4 + p])
    started += chunks

    first = [offs[0, 32 + lax.rem(at[Y] + 4 - p, 4)] for p in range(4)]

    def put(t, carry):
        row = t * 8
        value = None
        for p in range(4):
            u = lax.min(lax.max(row - first[p] + 8, 0), cap + 8)
            got = z[p, pl.ds(u, 8), :]
            value = got if value is None else value + got
        full0[pl.ds(pl.multiple_of(row, 8), 8), :] = value
        return carry

    lax.fori_loop(0, books // 8, put, 0, unroll=8)
    pair = send(full0, full1, psend, precv, C, 1)
    started.append(pair)

    core = at[C]

    def gather(h):
        def some(g, carry):
            k0 = (g // 4) * 64 + core * 32 + lax.rem(g, 4) * 8
            for r in range(8):
                book = owner[k0 + r]
                own[h, pl.ds(g * 8 + r, 1), :] = full[h][pl.ds(book, 1), :]
            return carry

        lax.fori_loop(0, own.shape[1] // 8, some, 0, unroll=2)

    fetch.wait()
    gather(0)
    pair.wait_recv()
    gather(1)

    sums = [full[h][...].reshape(books // 8, 8, LANES).sum(axis=0).sum(axis=0, keepdims=True) for h in (0, 1)]
    square = (sums[0] * sums[0] + sums[1] * sums[1]).sum(axis=1, keepdims=True)
    pieces = books // LANES + 1
    each = pieces // 3
    gram[pieces - 1] = jnp.broadcast_to(square, (4, 4, 4, 8, LANES))

    def pick(ref, dim, index):
        return ref.at[(slice(None),) * dim + (index,)]

    def scatter(stage, n, source, lands):
        name, dim = COLOURS[n // each][stage]
        copies = []
        for p in (2, 1, 3):
            copies.append(
                (p, send(
                    pick(source, dim, peer(name, p)), lands.at[n, p - 1],
                    rsend.at[stage, n, p - 1], rrecv.at[stage, n, p - 1], name, p,
                ))
            )
        return copies

    def reduce(stage, n, source, lands, copies):
        name, dim = COLOURS[n // each][stage]
        value = pick(source, dim, at[name])[...]
        for p, copy in copies:
            copy.wait_recv()
            value = value + lands[n, p - 1]
            started.append(copy)
        return value

    order = [each * c + q for q in range(each) for c in range(3)]
    flying = {}
    a0h, a0l = split(own[0])
    a1h, a1l = split(own[1])
    left = jnp.concatenate([a0h, a1h, a0h, a1h, a0l, a1l], axis=1)
    for n in order:
        if n < pieces - 1:
            rows = slice(LANES * n, LANES * (n + 1))
            b0h, b0l = split(full0[rows, :])
            b1h, b1l = split(full1[rows, :])
            right = jnp.concatenate([b0h, b1h, b0l, b1l, b0h, b1h], axis=1)
            got = lax.dot_general(
                left, right, (((1,), (1,)), ((), ())), preferred_element_type=jnp.float32
            )
            gram[n] = got.reshape(4, 4, 4, 8, LANES)
        flying[n] = scatter(0, n, gram.at[n], land1)
    for n in order:
        part1[n] = reduce(0, n, gram.at[n], land1, flying[n])
        flying[n] = scatter(1, n, part1.at[n], land2)
    for n in order:
        part2[n] = reduce(1, n, part1.at[n], land2, flying[n])
        flying[n] = scatter(2, n, part2.at[n], land3)
    done = {n: reduce(2, n, part2.at[n], land3, flying[n]) for n in order}
    row = None
    for n in range(pieces - 1):
        value = done[n] / total
        cov[:, LANES * n : LANES * (n + 1)] = value
        row = value if row is None else row + value
    variance = done[pieces - 1] / total
    con[...] = row.sum(axis=1, keepdims=True) / jnp.sqrt(variance)
    for copy in started:
        copy.wait_send()


def exchange(xc, facts, owner, cap, total, collective):
    books = xc.shape[1]
    f32 = jnp.float32
    pieces = books // LANES + 1
    rows = books // 128
    dma = pltpu.SemaphoreType.DMA
    return pl.pallas_call(
        functools.partial(exchange_body, cap, total),
        out_shape=(
            jax.ShapeDtypeStruct((rows, books), f32),
            jax.ShapeDtypeStruct((rows, LANES), f32),
        ),
        in_specs=[
            pl.BlockSpec(memory_space=pltpu.SMEM),
            pl.BlockSpec(memory_space=pl.ANY),
            pl.BlockSpec(memory_space=pltpu.VMEM),
        ],
        out_specs=[pl.BlockSpec(memory_space=pltpu.VMEM)] * 2,
        scratch_shapes=[
            pltpu.SMEM(owner.shape, jnp.int32),
            pltpu.VMEM((3, cap, LANES), f32),
            pltpu.VMEM((3, 8, cap), f32),
            pltpu.VMEM((6, 8, cap), f32),
            pltpu.VMEM((8, 8, cap), f32),
            pltpu.VMEM((4, cap + 16, LANES), f32),
            pltpu.VMEM((books, LANES), f32),
            pltpu.VMEM((books, LANES), f32),
            pltpu.VMEM((2, books // 2, LANES), f32),
            pltpu.VMEM((pieces, 4, 4, 4, 8, LANES), f32),
            pltpu.VMEM((pieces, 3, 4, 4, 8, LANES), f32),
            pltpu.VMEM((pieces, 3, 4, 8, LANES), f32),
            pltpu.VMEM((pieces, 3, 8, LANES), f32),
            pltpu.VMEM((pieces, 4, 4, 8, LANES), f32),
            pltpu.VMEM((pieces, 4, 8, LANES), f32),
            dma((3,)), dma((3,)), dma((13,)), dma((13,)), dma, dma,
            dma((3, pieces, 3)), dma((3, pieces, 3)), dma,
        ],
        name="exchange_%d" % cap,
        compiler_params=pltpu.CompilerParams(
            collective_id=collective, has_side_effects=True, vmem_limit_bytes=40 << 20
        ),
    )(facts, owner, xc)


def per_device(losses, book_sizes, owner_books):
    rows, places = losses.shape
    books = book_sizes.shape[0]
    total = rows * lax.axis_size(SCEN)
    xc, facts = segment_sums(losses, book_sizes)
    fits = facts[0, 64] < SHORT
    cov, con = lax.cond(
        fits,
        lambda *a: exchange(*a, SHORT, total, 1),
        lambda *a: exchange(*a, books, total, 2),
        xc, facts, owner_books,
    )
    return cov, con[:, 0]


def solution(mesh):
    grid = Mesh(mesh.devices.reshape(4, 4, 2, mesh.shape["pos"]), SCEN_POS)
    return jax.shard_map(
        per_device,
        mesh=grid,
        in_specs=(P(SCEN, Y), P(), P()),
        out_specs=(P(SCEN_POS, None), P(SCEN_POS)),
        check_vma=False,
    )
```

```python
import functools

import jax
import jax.numpy as jnp
from jax import lax
from jax.experimental import pallas as pl
from jax.experimental.pallas import tpu as pltpu
from jax.sharding import Mesh
from jax.sharding import PartitionSpec as P

LANES = 128
TILE = 256
SHORT = 384
WINDOW = 128
PAD = 32
GROUPS = ((0, 1), (1, 3), (3, 4))
X, Z, C, Y = "scen_0", "scen_1", "scen_2", "pos"
SCEN = (X, Z, C)
SCEN_POS = (X, Z, C, Y)
COLOURS = (((X, 0), (Z, 0), (Y, 0)), ((Z, 1), (Y, 1), (X, 0)), ((Y, 2), (X, 0), (Z, 0)))


def to_column(row):
    return jnp.broadcast_to(row, (LANES, LANES)).T


def fill_starts(sizes_ref, col, books):
    f32 = jnp.float32
    sizes = sizes_ref[...].astype(f32)
    down = lax.broadcasted_iota(jnp.int32, (LANES, LANES), 0)
    across = lax.broadcasted_iota(jnp.int32, (LANES, LANES), 1)
    upper = jnp.where(down <= across, 1.0, 0.0).astype(f32)
    within = jnp.dot(sizes, upper, precision=lax.Precision.HIGHEST, preferred_element_type=f32)
    before = [jnp.zeros((1, LANES), f32)]
    for k in range(books // LANES - 1):
        before.append(before[-1] + within[k : k + 1, LANES - 1 : LANES])
    start = within - sizes + jnp.concatenate(before, axis=0)
    for k in range(books // LANES):
        col[LANES * k : LANES * (k + 1), :] = to_column(start[k : k + 1, :]).astype(jnp.int32)
    col[books:, :] = jnp.full((col.shape[0] - books, LANES), 1 << 24, jnp.int32)


def books_at(col, books, place):
    count = jnp.zeros((8, LANES), jnp.int32)
    for b in range(0, books, 8):
        count = count + jnp.where(col[b : b + 8, :] <= place, 1, 0)
    return jnp.sum(count, axis=0, keepdims=True) - 1


def segsum_body(blocks, sizes_ref, x_hbm, out_ref, facts_ref, kept, col, sems):
    books = out_ref.shape[1]
    places = x_hbm.shape[1]
    me = lax.axis_index(Y)
    f32 = jnp.float32
    copies = []
    for n, (at, width) in enumerate(blocks):
        piece = pl.ds(at, width)
        copies.append(pltpu.make_async_copy(x_hbm.at[:, piece], kept.at[:, piece], sems.at[n]))
        copies[-1].start()

    fill_starts(sizes_ref, col, books)

    lane = lax.broadcasted_iota(jnp.int32, (1, LANES), 1)
    place = jnp.zeros((1, LANES), jnp.int32)
    for n, (at, width) in enumerate(blocks):
        place = jnp.where(lane == n, me * places + at, place)
        place = jnp.where(lane == 16 + n, me * places + at + width - 1, place)
    for j in range(4):
        place = jnp.where(lane == 32 + j, j * places, place)
        place = jnp.where(lane == 48 + j, j * places + places - 1, place)
    facts = books_at(col, books, place)
    facts = jnp.where((lane >= 32) & (lane < 48), facts // 8 * 8, facts)

    def fact(i):
        return jnp.sum(jnp.where(lane == i, facts, 0))

    facts_ref[...] = facts
    mine = fact(32 + me)
    spans = [((fact(n) - mine) // TILE, (fact(16 + n) - mine) // TILE) for n in range(len(blocks))]
    out_ref[...] = jnp.zeros_like(out_ref)

    lanes = lax.broadcasted_iota(jnp.int32, (TILE, LANES), 1)
    for n, (at, width) in enumerate(blocks):
        base = me * places + at
        copies[n].wait()

        def add_tile(t, carry):
            r0 = pl.multiple_of(t * TILE, TILE)
            g0 = pl.multiple_of(mine + r0, 8)
            begin = col[pl.ds(g0, TILE), :] - base
            end = col[pl.ds(g0 + 1, TILE), :] - base
            parts = []
            for l in range(0, width, LANES):
                inside = (lanes + l >= begin) & (lanes + l < end)
                parts.append(jnp.where(inside, 1.0, 0.0).astype(jnp.bfloat16))
            sums = lax.dot_general(
                jnp.concatenate(parts, axis=1), kept[:, at : at + width],
                (((1,), (1,)), ((), ())), preferred_element_type=f32,
            )
            for c in range(out_ref.shape[0]):
                out_ref[c, pl.ds(r0, TILE), :] += sums[:, LANES * c : LANES * (c + 1)]
            return carry

        lax.fori_loop(spans[n][0], spans[n][1] + 1, add_tile, 0)


def segment_sums(losses, sizes):
    rows, places = losses.shape
    books = sizes.shape[0]
    widths = [places // 4] * 3 + [places // 8] * 2
    blocks = tuple((sum(widths[:n]), w) for n, w in enumerate(widths))
    return pl.pallas_call(
        functools.partial(segsum_body, blocks),
        out_shape=(
            jax.ShapeDtypeStruct((rows // LANES, books, LANES), jnp.float32),
            jax.ShapeDtypeStruct((1, LANES), jnp.int32),
        ),
        in_specs=[pl.BlockSpec(memory_space=pltpu.VMEM), pl.BlockSpec(memory_space=pl.ANY)],
        out_specs=[pl.BlockSpec(memory_space=pltpu.VMEM)] * 2,
        scratch_shapes=[
            pltpu.VMEM((rows, places), jnp.bfloat16),
            pltpu.VMEM((2 * books + TILE, LANES), jnp.int32),
            pltpu.SemaphoreType.DMA((len(blocks),)),
        ],
        name="segment_sums",
        compiler_params=pltpu.CompilerParams(vmem_limit_bytes=48 << 20),
    )(sizes.reshape(books // LANES, LANES), losses)


def split(x):
    high = x.astype(jnp.bfloat16)
    return high, (x - high.astype(jnp.float32)).astype(jnp.bfloat16)


def exchange_body(cap, total, fused, *refs):
    if fused:
        sizes, owners, x_hbm, cov, con, facts_ref = refs[:6]
        kept, col, masks, sums_at, xc, csem = refs[6:12]
        refs = refs[12:]
    else:
        offs, owners, xc, cov, con = refs[:5]
        refs = refs[5:]
    (
        owner, land, vsum, xvec, yvec, z, full0, full1, own, gram, land1, land2, land3, part1, part2,
        ysend, yrecv, vsend, vrecv, psend, precv, rsend, rrecv, osem,
    ) = refs
    at = {name: lax.axis_index(name) for name in SCEN_POS}
    size = {X: 4, Z: 4, C: 2, Y: 4}
    full = (full0, full1)
    books = full0.shape[0]

    def peer(name, p):
        return lax.rem(at[name] + p, size[name])

    fetch = pltpu.make_async_copy(owners, owner, osem)
    fetch.start()
    around = [(a, b) for a in range(size[X]) for b in range(size[Z]) if a or b]
    along = [(d, p) for p in (2, 1, 3, 0) for d in range(size[C]) if d or p]
    others = [{X: peer(X, a), Z: peer(Z, b)} for a, b in around]
    others += [{C: peer(C, d), Y: peer(Y, p)} for d, p in along]
    if fused:
        loads = []
        for n, p in enumerate((2, 1, 3, 0)):
            rows = pl.ds(pl.multiple_of(peer(Y, p) * LANES, LANES), LANES)
            loads.append(
                pltpu.make_async_copy(
                    x_hbm.at[rows, :], kept.at[pl.ds(LANES * n, LANES), :], csem.at[n]
                )
            )
            loads[-1].start()
    barrier = pltpu.get_barrier_semaphore()
    for other in others:
        pl.semaphore_signal(barrier, inc=1, device_id=other, device_id_type=pl.DeviceIdType.MESH)
    pl.semaphore_wait(barrier, len(others))

    def send_to(src, dst, s, r, device):
        copy = pltpu.make_async_remote_copy(
            src_ref=src,
            dst_ref=dst,
            send_sem=s,
            recv_sem=r,
            device_id=device,
            device_id_type=pl.DeviceIdType.MESH,
        )
        copy.start()
        return copy

    def send(src, dst, s, r, name, p):
        return send_to(src, dst, s, r, {name: peer(name, p)})

    started = []
    zero = jnp.zeros((PAD, LANES), jnp.float32)
    chunks = []

    def send_chunk(slot):
        p = (2, 1, 3)[slot]
        source = xc.at[slot] if fused else xc.at[peer(Y, p), pl.ds(0, cap), :]
        chunks.append(send(source, land.at[p - 1], ysend.at[p - 1], yrecv.at[p - 1], Y, p))

    if fused:
        places = x_hbm.shape[1]
        width = masks.shape[1] // sums_at.shape[1]
        parts = places // width
        fill_starts(sizes, col, books)
        lane = lax.broadcasted_iota(jnp.int32, (1, LANES), 1)
        blocks = 4 * parts
        step = jnp.where(lane < blocks, width, places)
        place = jnp.where(lane < blocks, lane, lane - blocks) * step
        early = books_at(col, books, place) // 8 * 8
        span = books_at(col, books, place + step - 1) - early
        spare = jnp.where(
            lane < blocks, WINDOW - 1 - span, jnp.where(lane < blocks + 4, cap - 1 - span, 0)
        )
        facts_ref[...] = jnp.broadcast_to(jnp.min(spare, axis=1, keepdims=True), (1, LANES))

        def fact(i):
            return jnp.sum(jnp.where(lane == i, early, 0))

        first = [fact(blocks + lax.rem(at[Y] + 4 - p, 4)) for p in range(4)]
        begins = [fact(at[Y] * parts + i) for i in range(parts)]
        lanes = lax.broadcasted_iota(jnp.int32, (WINDOW, LANES), 1)
        for i in range(parts):
            base = at[Y] * places + i * width
            low = col[pl.ds(begins[i], WINDOW), :] - base
            high = col[pl.ds(begins[i] + 1, WINDOW), :] - base
            for l in range(0, width, LANES):
                inside = (lanes + l >= low) & (lanes + l < high)
                masks[:, i * width + l : i * width + l + LANES] = jnp.where(inside, 1.0, 0.0).astype(
                    jnp.bfloat16
                )
            for q in range(4):
                sums_at[q, i, 0:PAD, :] = zero
                sums_at[q, i, PAD + WINDOW :, :] = zero
        for a, b in GROUPS:
            for q in range(a, b):
                loads[q].wait()
            for i in range(parts):
                piece = slice(i * width, (i + 1) * width)
                got = lax.dot_general(
                    masks[:, piece], kept[LANES * a : LANES * b, piece],
                    (((1,), (1,)), ((), ())), preferred_element_type=jnp.float32,
                )
                for q in range(a, b):
                    sums_at[q, i, PAD : PAD + WINDOW, :] = got[:, LANES * (q - a) : LANES * (q - a + 1)]

            def combine(t, carry):
                for q in range(a, b):
                    value = None
                    for i in range(parts):
                        u = lax.min(lax.max(t * PAD - (begins[i] - first[0]) + PAD, 0), WINDOW + PAD)
                        got = sums_at[q, i, pl.ds(u, PAD), :]
                        value = got if value is None else value + got
                    xc[q, pl.ds(pl.multiple_of(t * PAD, PAD), PAD), :] = value
                return carry

            lax.fori_loop(0, cap // PAD, combine, 0, unroll=2)
            for q in range(a, min(b, 3)):
                send_chunk(q)
    else:
        first = [offs[0, 32 + lax.rem(at[Y] + 4 - p, 4)] for p in range(4)]
        for q in range(3):
            send_chunk(q)

    for b in range(0, cap, LANES):
        rows = slice(b, b + LANES)
        block = (xc[0, rows, :] + xc[1, rows, :]) + (xc[2, rows, :] + xc[3, rows, :])
        vsum[0, :, rows] = block.T.sum(axis=0, keepdims=True)
    xcopies = []
    for n, (a, b) in enumerate(around):
        xcopies.append(
            send_to(vsum.at[0], xvec.at[n], vsend.at[n], vrecv.at[n], {X: peer(X, a), Z: peer(Z, b)})
        )
    value = vsum[0]
    for n, copy in enumerate(xcopies):
        copy.wait_recv()
        value = value + xvec[n]
    vsum[1] = value
    started += xcopies
    ycopies = {}
    for n, (d, p) in enumerate(along):
        slot = len(around) + n
        ycopies[d, p] = send_to(
            vsum.at[1], yvec.at[4 * d + p], vsend.at[slot], vrecv.at[slot],
            {C: peer(C, d), Y: peer(Y, p)},
        )
    started += ycopies.values()


    def centre(p, values, sums):
        z[p, 0:PAD, :] = zero
        z[p, cap + PAD :, :] = zero
        mean = sums / total
        for b in range(0, cap, LANES):
            z[p, PAD + b : PAD + b + LANES, :] = values[b : b + LANES, :] - to_column(
                mean[:, b : b + LANES]
            )

    ycopies[1, 0].wait_recv()
    centre(0, xc.at[3] if fused else xc.at[at[Y]], vsum[1] + yvec[4])
    for n, p in ((1, 1), (2, 3), (0, 2)):
        ycopies[0, p].wait_recv()
        ycopies[1, p].wait_recv()
        chunks[n].wait_recv()
        centre(p, land.at[p - 1], yvec[p] + yvec[4 + p])
    started += chunks

    def put(t, carry):
        row = t * PAD
        value = None
        for p in range(4):
            u = lax.min(lax.max(row - first[p] + PAD, 0), cap + PAD)
            got = z[p, pl.ds(u, PAD), :]
            value = got if value is None else value + got
        full0[pl.ds(pl.multiple_of(row, PAD), PAD), :] = value
        return carry

    lax.fori_loop(0, books // PAD, put, 0, unroll=2)
    pair = send(full0, full1, psend, precv, C, 1)
    started.append(pair)

    core = at[C]

    def gather(h):
        def some(g, carry):
            k0 = (g // 4) * 64 + core * 32 + lax.rem(g, 4) * 8
            for r in range(8):
                book = owner[k0 + r]
                own[h, pl.ds(g * 8 + r, 1), :] = full[h][pl.ds(book, 1), :]
            return carry

        lax.fori_loop(0, own.shape[1] // 8, some, 0, unroll=2)

    fetch.wait()
    gather(0)
    pair.wait_recv()
    gather(1)

    sums = [full[h][...].reshape(books // 8, 8, LANES).sum(axis=0).sum(axis=0, keepdims=True) for h in (0, 1)]
    square = (sums[0] * sums[0] + sums[1] * sums[1]).sum(axis=1, keepdims=True)
    pieces = books // LANES + 1
    each = pieces // 3
    gram[pieces - 1] = jnp.broadcast_to(square, (4, 4, 4, 8, LANES))

    def pick(ref, dim, index):
        return ref.at[(slice(None),) * dim + (index,)]

    def scatter(stage, n, source, lands):
        name, dim = COLOURS[n // each][stage]
        copies = []
        for p in (2, 1, 3):
            copies.append(
                (p, send(
                    pick(source, dim, peer(name, p)), lands.at[n, p - 1],
                    rsend.at[stage, n, p - 1], rrecv.at[stage, n, p - 1], name, p,
                ))
            )
        return copies

    def reduce(stage, n, source, lands, copies):
        name, dim = COLOURS[n // each][stage]
        value = pick(source, dim, at[name])[...]
        for p, copy in copies:
            copy.wait_recv()
            value = value + lands[n, p - 1]
            started.append(copy)
        return value

    order = [each * c + q for q in range(each) for c in range(3)]
    flying = {}
    a0h, a0l = split(own[0])
    a1h, a1l = split(own[1])
    left = jnp.concatenate([a0h, a1h, a0h, a1h, a0l, a1l], axis=1)
    for n in order:
        if n < pieces - 1:
            rows = slice(LANES * n, LANES * (n + 1))
            b0h, b0l = split(full0[rows, :])
            b1h, b1l = split(full1[rows, :])
            right = jnp.concatenate([b0h, b1h, b0l, b1l, b0h, b1h], axis=1)
            got = lax.dot_general(
                left, right, (((1,), (1,)), ((), ())), preferred_element_type=jnp.float32
            )
            gram[n] = got.reshape(4, 4, 4, 8, LANES)
        flying[n] = scatter(0, n, gram.at[n], land1)
    for n in order:
        part1[n] = reduce(0, n, gram.at[n], land1, flying[n])
        flying[n] = scatter(1, n, part1.at[n], land2)
    for n in order:
        part2[n] = reduce(1, n, part1.at[n], land2, flying[n])
        flying[n] = scatter(2, n, part2.at[n], land3)
    done = {n: reduce(2, n, part2.at[n], land3, flying[n]) for n in order}
    row = None
    for n in range(pieces - 1):
        value = done[n] / total
        cov[:, LANES * n : LANES * (n + 1)] = value
        row = value if row is None else row + value
    variance = done[pieces - 1] / total
    con[...] = row.sum(axis=1, keepdims=True) / jnp.sqrt(variance)
    for copy in started:
        copy.wait_send()


def exchange(operands, owner, cap, total, collective, fused):
    books = owner.shape[0]
    f32 = jnp.float32
    pieces = books // LANES + 1
    rows = books // 128
    dma = pltpu.SemaphoreType.DMA
    out_shape = [
        jax.ShapeDtypeStruct((rows, books), f32),
        jax.ShapeDtypeStruct((rows, LANES), f32),
    ]
    vmem = pl.BlockSpec(memory_space=pltpu.VMEM)
    hbm = pl.BlockSpec(memory_space=pl.ANY)
    if fused:
        sizes, losses = operands
        operands = (sizes.reshape(books // LANES, LANES), owner, losses)
        in_specs = [vmem, hbm, hbm]
        out_shape.append(jax.ShapeDtypeStruct((1, LANES), jnp.int32))
        places = losses.shape[1]
        parts = places // 2048
        scratch = [
            pltpu.VMEM(losses.shape, losses.dtype),
            pltpu.VMEM((books + 2 * LANES, LANES), jnp.int32),
            pltpu.VMEM((WINDOW, places), losses.dtype),
            pltpu.VMEM((4, parts, WINDOW + 2 * PAD, LANES), f32),
            pltpu.VMEM((4, cap, LANES), f32),
            dma((4,)),
        ]
    else:
        facts, xc = operands
        operands = (facts, owner, xc)
        in_specs = [pl.BlockSpec(memory_space=pltpu.SMEM), hbm, vmem]
        scratch = []
    return pl.pallas_call(
        functools.partial(exchange_body, cap, total, fused),
        out_shape=out_shape,
        in_specs=in_specs,
        out_specs=[vmem] * len(out_shape),
        scratch_shapes=scratch + [
            pltpu.SMEM(owner.shape, jnp.int32),
            pltpu.VMEM((3, cap, LANES), f32),
            pltpu.VMEM((2, 1, cap), f32),
            pltpu.VMEM((15, 1, cap), f32),
            pltpu.VMEM((8, 1, cap), f32),
            pltpu.VMEM((4, cap + 2 * PAD, LANES), f32),
            pltpu.VMEM((books, LANES), f32),
            pltpu.VMEM((books, LANES), f32),
            pltpu.VMEM((2, books // 2, LANES), f32),
            pltpu.VMEM((pieces, 4, 4, 4, 8, LANES), f32),
            pltpu.VMEM((pieces, 3, 4, 4, 8, LANES), f32),
            pltpu.VMEM((pieces, 3, 4, 8, LANES), f32),
            pltpu.VMEM((pieces, 3, 8, LANES), f32),
            pltpu.VMEM((pieces, 4, 4, 8, LANES), f32),
            pltpu.VMEM((pieces, 4, 8, LANES), f32),
            dma((3,)), dma((3,)), dma((22,)), dma((22,)), dma, dma,
            dma((3, pieces, 3)), dma((3, pieces, 3)), dma,
        ],
        name="exchange_%d" % cap,
        compiler_params=pltpu.CompilerParams(
            collective_id=collective, has_side_effects=True, vmem_limit_bytes=56 << 20
        ),
    )(*operands)


def per_device(losses, book_sizes, owner_books):
    rows, places = losses.shape
    books = book_sizes.shape[0]
    total = rows * lax.axis_size(SCEN)
    cov, con, spare = exchange((book_sizes, losses), owner_books, SHORT, total, 1, True)

    def general(cov, con, losses, sizes, owner):
        xc, facts = segment_sums(losses, sizes)
        return tuple(exchange((facts, xc), owner, books, total, 2, False))

    cov, con = lax.cond(
        spare[0, 0] >= 0,
        lambda cov, con, *rest: (cov, con),
        general,
        cov, con, losses, book_sizes, owner_books,
    )
    return cov, con[:, 0]


def solution(mesh):
    grid = Mesh(mesh.devices.reshape(4, 4, 2, mesh.shape["pos"]), SCEN_POS)
    return jax.shard_map(
        per_device,
        mesh=grid,
        in_specs=(P(SCEN, Y), P(), P()),
        out_specs=(P(SCEN_POS, None), P(SCEN_POS)),
        check_vma=False,
    )
```

```python
import functools

import jax
import jax.numpy as jnp
from jax import lax
from jax.experimental import pallas as pl
from jax.experimental.pallas import tpu as pltpu
from jax.sharding import Mesh
from jax.sharding import PartitionSpec as P

LANES = 128
TILE = 256
SHORT = 384
WINDOW = 128
PAD = 32
GROUPS = ((0, 1), (1, 3), (3, 4))
X, Z, C, Y = "scen_0", "scen_1", "scen_2", "pos"
SCEN = (X, Z, C)
SCEN_POS = (X, Z, C, Y)
COLOURS = (((X, 0), (Z, 0), (Y, 0)), ((Z, 1), (Y, 1), (X, 0)), ((Y, 2), (X, 0), (Z, 0)))


def to_column(row):
    return jnp.broadcast_to(row, (LANES, LANES)).T


def fill_starts(sizes_ref, col, books):
    f32 = jnp.float32
    sizes = sizes_ref[...].astype(f32)
    down = lax.broadcasted_iota(jnp.int32, (LANES, LANES), 0)
    across = lax.broadcasted_iota(jnp.int32, (LANES, LANES), 1)
    upper = jnp.where(down <= across, 1.0, 0.0).astype(f32)
    within = jnp.dot(sizes, upper, precision=lax.Precision.HIGHEST, preferred_element_type=f32)
    before = [jnp.zeros((1, LANES), f32)]
    for k in range(books // LANES - 1):
        before.append(before[-1] + within[k : k + 1, LANES - 1 : LANES])
    start = within - sizes + jnp.concatenate(before, axis=0)
    for k in range(books // LANES):
        col[LANES * k : LANES * (k + 1), :] = to_column(start[k : k + 1, :]).astype(jnp.int32)
    col[books:, :] = jnp.full((col.shape[0] - books, LANES), 1 << 24, jnp.int32)


def books_at(col, books, place):
    count = jnp.zeros((8, LANES), jnp.int32)
    for b in range(0, books, 8):
        count = count + jnp.where(col[b : b + 8, :] <= place, 1, 0)
    return jnp.sum(count, axis=0, keepdims=True) - 1


def segsum_body(blocks, sizes_ref, x_hbm, out_ref, facts_ref, kept, col, sems):
    books = out_ref.shape[1]
    places = x_hbm.shape[1]
    me = lax.axis_index(Y)
    f32 = jnp.float32
    copies = []
    for n, (at, width) in enumerate(blocks):
        piece = pl.ds(at, width)
        copies.append(pltpu.make_async_copy(x_hbm.at[:, piece], kept.at[:, piece], sems.at[n]))
        copies[-1].start()

    fill_starts(sizes_ref, col, books)

    lane = lax.broadcasted_iota(jnp.int32, (1, LANES), 1)
    place = jnp.zeros((1, LANES), jnp.int32)
    for n, (at, width) in enumerate(blocks):
        place = jnp.where(lane == n, me * places + at, place)
        place = jnp.where(lane == 16 + n, me * places + at + width - 1, place)
    for j in range(4):
        place = jnp.where(lane == 32 + j, j * places, place)
        place = jnp.where(lane == 48 + j, j * places + places - 1, place)
    facts = books_at(col, books, place)
    facts = jnp.where((lane >= 32) & (lane < 48), facts // 8 * 8, facts)

    def fact(i):
        return jnp.sum(jnp.where(lane == i, facts, 0))

    facts_ref[...] = facts
    mine = fact(32 + me)
    spans = [((fact(n) - mine) // TILE, (fact(16 + n) - mine) // TILE) for n in range(len(blocks))]
    out_ref[...] = jnp.zeros_like(out_ref)

    lanes = lax.broadcasted_iota(jnp.int32, (TILE, LANES), 1)
    for n, (at, width) in enumerate(blocks):
        base = me * places + at
        copies[n].wait()

        def add_tile(t, carry):
            r0 = pl.multiple_of(t * TILE, TILE)
            g0 = pl.multiple_of(mine + r0, 8)
            begin = col[pl.ds(g0, TILE), :] - base
            end = col[pl.ds(g0 + 1, TILE), :] - base
            parts = []
            for l in range(0, width, LANES):
                inside = (lanes + l >= begin) & (lanes + l < end)
                parts.append(jnp.where(inside, 1.0, 0.0).astype(jnp.bfloat16))
            sums = lax.dot_general(
                jnp.concatenate(parts, axis=1), kept[:, at : at + width],
                (((1,), (1,)), ((), ())), preferred_element_type=f32,
            )
            for c in range(out_ref.shape[0]):
                out_ref[c, pl.ds(r0, TILE), :] += sums[:, LANES * c : LANES * (c + 1)]
            return carry

        lax.fori_loop(spans[n][0], spans[n][1] + 1, add_tile, 0)


def segment_sums(losses, sizes):
    rows, places = losses.shape
    books = sizes.shape[0]
    widths = [places // 4] * 3 + [places // 8] * 2
    blocks = tuple((sum(widths[:n]), w) for n, w in enumerate(widths))
    return pl.pallas_call(
        functools.partial(segsum_body, blocks),
        out_shape=(
            jax.ShapeDtypeStruct((rows // LANES, books, LANES), jnp.float32),
            jax.ShapeDtypeStruct((1, LANES), jnp.int32),
        ),
        in_specs=[pl.BlockSpec(memory_space=pltpu.VMEM), pl.BlockSpec(memory_space=pl.ANY)],
        out_specs=[pl.BlockSpec(memory_space=pltpu.VMEM)] * 2,
        scratch_shapes=[
            pltpu.VMEM((rows, places), jnp.bfloat16),
            pltpu.VMEM((2 * books + TILE, LANES), jnp.int32),
            pltpu.SemaphoreType.DMA((len(blocks),)),
        ],
        name="segment_sums",
        compiler_params=pltpu.CompilerParams(vmem_limit_bytes=48 << 20),
    )(sizes.reshape(books // LANES, LANES), losses)


def split(x):
    high = x.astype(jnp.bfloat16)
    return high, (x - high.astype(jnp.float32)).astype(jnp.bfloat16)


def exchange_body(cap, total, fused, *refs):
    if fused:
        sizes, owners, x_hbm, cov, con, facts_ref = refs[:6]
        kept, col, masks, sums_at, xc, csem = refs[6:12]
        refs = refs[12:]
    else:
        offs, owners, xc, cov, con = refs[:5]
        refs = refs[5:]
    (
        owner, land, vsum, xvec, yvec, z, zmean, full0, full1, mean, own, gram, relay, land1, land2, land3,
        part1, part2, ysend, yrecv, vsend, vrecv, psend, precv, esend, erecv, rsend, rrecv, osem,
    ) = refs
    at = {name: lax.axis_index(name) for name in SCEN_POS}
    size = {X: 4, Z: 4, C: 2, Y: 4}
    full = (full0, full1)
    books = full0.shape[0]

    def peer(name, p):
        return lax.rem(at[name] + p, size[name])

    fetch = pltpu.make_async_copy(owners, owner, osem)
    fetch.start()
    around = [(a, b) for a in range(size[X]) for b in range(size[Z]) if a or b]
    along = [(d, p) for p in (2, 1, 3, 0) for d in range(size[C]) if d or p]
    others = [{X: peer(X, a), Z: peer(Z, b)} for a, b in around]
    others += [{C: peer(C, d), Y: peer(Y, p)} for d, p in along]
    if fused:
        loads = []
        for n, p in enumerate((2, 1, 3, 0)):
            rows = pl.ds(pl.multiple_of(peer(Y, p) * LANES, LANES), LANES)
            loads.append(
                pltpu.make_async_copy(
                    x_hbm.at[rows, :], kept.at[pl.ds(LANES * n, LANES), :], csem.at[n]
                )
            )
            loads[-1].start()
    barrier = pltpu.get_barrier_semaphore()
    for other in others:
        pl.semaphore_signal(barrier, inc=1, device_id=other, device_id_type=pl.DeviceIdType.MESH)
    pl.semaphore_wait(barrier, len(others))

    def send_to(src, dst, s, r, device):
        copy = pltpu.make_async_remote_copy(
            src_ref=src,
            dst_ref=dst,
            send_sem=s,
            recv_sem=r,
            device_id=device,
            device_id_type=pl.DeviceIdType.MESH,
        )
        copy.start()
        return copy

    def send(src, dst, s, r, name, p):
        return send_to(src, dst, s, r, {name: peer(name, p)})

    started = []
    zero = jnp.zeros((PAD, LANES), jnp.float32)
    chunks = []

    def send_chunk(slot):
        p = (2, 1, 3)[slot]
        source = xc.at[slot] if fused else xc.at[peer(Y, p), pl.ds(0, cap), :]
        chunks.append(send(source, land.at[p - 1], ysend.at[p - 1], yrecv.at[p - 1], Y, p))

    if fused:
        places = x_hbm.shape[1]
        width = masks.shape[1] // sums_at.shape[1]
        parts = places // width
        fill_starts(sizes, col, books)
        lane = lax.broadcasted_iota(jnp.int32, (1, LANES), 1)
        blocks = 4 * parts
        step = jnp.where(lane < blocks, width, places)
        place = jnp.where(lane < blocks, lane, lane - blocks) * step
        early = books_at(col, books, place) // 8 * 8
        span = books_at(col, books, place + step - 1) - early
        spare = jnp.where(
            lane < blocks, WINDOW - 1 - span, jnp.where(lane < blocks + 4, cap - 1 - span, 0)
        )
        facts_ref[...] = jnp.broadcast_to(jnp.min(spare, axis=1, keepdims=True), (1, LANES))

        def fact(i):
            return jnp.sum(jnp.where(lane == i, early, 0))

        first = [fact(blocks + lax.rem(at[Y] + 4 - p, 4)) for p in range(4)]
        begins = [fact(at[Y] * parts + i) for i in range(parts)]
        lanes = lax.broadcasted_iota(jnp.int32, (WINDOW, LANES), 1)

        def member(i):
            base = at[Y] * places + i * width
            low = col[pl.ds(begins[i], WINDOW), :] - base
            high = col[pl.ds(begins[i] + 1, WINDOW), :] - base
            tiles = []
            for l in range(0, width, LANES):
                inside = (lanes + l >= low) & (lanes + l < high)
                tiles.append(jnp.where(inside, 1.0, 0.0).astype(jnp.bfloat16))
            return jnp.concatenate(tiles, axis=1)

        for i in range(parts):
            for q in range(4):
                sums_at[q, i, 0:PAD, :] = zero
                sums_at[q, i, PAD + WINDOW :, :] = zero
        for a, b in GROUPS:
            for q in range(a, b):
                loads[q].wait()
            for i in range(parts):
                piece = slice(i * width, (i + 1) * width)
                if a == 0:
                    chosen = member(i)
                    masks[:, piece] = chosen
                else:
                    chosen = masks[:, piece]
                got = lax.dot_general(
                    chosen, kept[LANES * a : LANES * b, piece],
                    (((1,), (1,)), ((), ())), preferred_element_type=jnp.float32,
                )
                for q in range(a, b):
                    sums_at[q, i, PAD : PAD + WINDOW, :] = got[:, LANES * (q - a) : LANES * (q - a + 1)]

            def combine(t, carry):
                for q in range(a, b):
                    value = None
                    for i in range(parts):
                        u = lax.min(lax.max(t * PAD - (begins[i] - first[0]) + PAD, 0), WINDOW + PAD)
                        got = sums_at[q, i, pl.ds(u, PAD), :]
                        value = got if value is None else value + got
                    xc[q, pl.ds(pl.multiple_of(t * PAD, PAD), PAD), :] = value
                return carry

            lax.fori_loop(0, cap // PAD, combine, 0, unroll=2)
            for q in range(a, min(b, 3)):
                send_chunk(q)
    else:
        first = [offs[0, 32 + lax.rem(at[Y] + 4 - p, 4)] for p in range(4)]
        for q in range(3):
            send_chunk(q)

    for b in range(0, cap, LANES):
        rows = slice(b, b + LANES)
        block = (xc[0, rows, :] + xc[1, rows, :]) + (xc[2, rows, :] + xc[3, rows, :])
        vsum[0, :, rows] = block.T.sum(axis=0, keepdims=True)
    xcopies = []
    for n, (a, b) in enumerate(around):
        xcopies.append(
            send_to(vsum.at[0], xvec.at[n], vsend.at[n], vrecv.at[n], {X: peer(X, a), Z: peer(Z, b)})
        )
    value = vsum[0]
    for n, copy in enumerate(xcopies):
        copy.wait_recv()
        value = value + xvec[n]
    vsum[1] = value
    started += xcopies
    ycopies = {}
    for n, (d, p) in enumerate(along):
        slot = len(around) + n
        ycopies[d, p] = send_to(
            vsum.at[1], yvec.at[4 * d + p], vsend.at[slot], vrecv.at[slot],
            {C: peer(C, d), Y: peer(Y, p)},
        )
    started += ycopies.values()


    for p in range(4):
        for ref in (z, zmean):
            ref[p, 0:PAD, :] = zero
            ref[p, cap + PAD :, :] = zero
    z[0, PAD : PAD + cap, :] = xc[3] if fused else xc[at[Y], 0:cap, :]
    for copy, p in zip(chunks, (2, 1, 3)):
        copy.wait_recv()
        z[p, PAD : PAD + cap, :] = land[p - 1]
    started += chunks

    def place_books(source, target):
        def put(t, carry):
            row = t * PAD
            value = None
            for p in range(4):
                u = lax.min(lax.max(row - first[p] + PAD, 0), cap + PAD)
                got = source[p, pl.ds(u, PAD), :]
                value = got if value is None else value + got
            target[pl.ds(pl.multiple_of(row, PAD), PAD), :] = value
            return carry

        lax.fori_loop(0, books // PAD, put, 0, unroll=2)

    place_books(z, full0)
    pair = send(full0, full1, psend, precv, C, 1)
    started.append(pair)

    core = at[C]

    def gather(source, h):
        def some(g, carry):
            k0 = (g // 4) * 64 + core * 32 + lax.rem(g, 4) * 8
            for r in range(8):
                book = owner[k0 + r]
                own[h, pl.ds(g * 8 + r, 1), :] = source[pl.ds(book, 1), :]
            return carry

        lax.fori_loop(0, own.shape[1] // 8, some, 0, unroll=2)

    fetch.wait()
    gather(full0, 0)

    for p in range(4):
        sums = vsum[1] if p == 0 else None
        for d in (0, 1):
            if d or p:
                ycopies[d, p].wait_recv()
                sums = yvec[4 * d + p] if sums is None else sums + yvec[4 * d + p]
        average = sums / total
        for b in range(0, cap, LANES):
            zmean[p, PAD + b : PAD + b + LANES, :] = to_column(average[:, b : b + LANES])
    place_books(zmean, mean)
    gather(mean, 2)
    pair.wait_recv()
    gather(full1, 1)

    pieces = books // LANES + 1
    each = pieces // 3

    def pick(ref, dim, index):
        return ref.at[(slice(None),) * dim + (index,)]

    def half(n, index, h):
        dim = COLOURS[n // each][0][1]
        some = pl.ds(2 * h, 2)
        where = [(index, some), (some, index), (some, slice(None), index)][dim]
        return gram.at[(n, *where)]

    def first_out(n):
        name = COLOURS[n // each][0][0]
        ahead, behind = peer(name, 1), peer(name, 3)
        copies = []
        for k, (index, h, target, p) in enumerate((
            (peer(name, 2), 0, relay.at[n, 0], 1),
            (peer(name, 2), 1, relay.at[n, 1], 3),
            (ahead, 1, land1.at[n, 0, pl.ds(2, 2)], 1),
            (behind, 0, land1.at[n, 1, pl.ds(0, 2)], 3),
        )):
            copies.append(send(half(n, index, h), target, esend.at[n, k], erecv.at[n, k], name, p))
        return copies

    def first_relay(n, copies):
        name = COLOURS[n // each][0][0]
        for h, p in ((0, 1), (1, 3)):
            copies[h].wait_recv()
            relay[n, h] = relay[n, h] + half(n, peer(name, p), h)[...]
            copies.append(
                send(
                    relay.at[n, h], land1.at[n, h, pl.ds(2 * h, 2)],
                    esend.at[n, 4 + h], erecv.at[n, 4 + h], name, p,
                )
            )

    def first_sum(n, copies):
        name, dim = COLOURS[n // each][0]
        for copy in copies[2:]:
            copy.wait_recv()
        started.extend(copies)
        return pick(gram.at[n], dim, at[name])[...] + (land1[n, 0] + land1[n, 1])

    def scatter(stage, n, source, lands):
        name, dim = COLOURS[n // each][stage]
        copies = []
        for p in (2, 1, 3):
            copies.append(
                (p, send(
                    pick(source, dim, peer(name, p)), lands.at[n, p - 1],
                    rsend.at[stage - 1, n, p - 1], rrecv.at[stage - 1, n, p - 1], name, p,
                ))
            )
        return copies

    def reduce(stage, n, source, lands, copies):
        name, dim = COLOURS[n // each][stage]
        value = pick(source, dim, at[name])[...]
        for p, copy in copies:
            copy.wait_recv()
            value = value + lands[n, p - 1]
            started.append(copy)
        return value

    order = [each * c + q for q in range(each) for c in range(3)]
    flying = {}
    a0h, a0l = split(own[0] - own[2])
    a1h, a1l = split(own[1] - own[2])
    left = jnp.concatenate([a0h, a1h, a0h, a1h, a0l, a1l], axis=1)
    for n in order:
        if n < pieces - 1:
            rows = slice(LANES * n, LANES * (n + 1))
            b0h, b0l = split(full0[rows, :] - mean[rows, :])
            b1h, b1l = split(full1[rows, :] - mean[rows, :])
            right = jnp.concatenate([b0h, b1h, b0l, b1l, b0h, b1h], axis=1)
            got = lax.dot_general(
                left, right, (((1,), (1,)), ((), ())), preferred_element_type=jnp.float32
            )
            gram[n] = got.reshape(4, 4, 4, 8, LANES)
        else:
            square = None
            for ref in (full0, full1):
                whole = (ref[...] - mean[...]).reshape(books // 8, 8, LANES).sum(axis=0)
                whole = whole.sum(axis=0, keepdims=True)
                square = whole * whole if square is None else square + whole * whole
            square = square.sum(axis=1, keepdims=True)
            gram[n] = jnp.broadcast_to(square, (4, 4, 4, 8, LANES))
        flying[n] = first_out(n)
    for n in order:
        first_relay(n, flying[n])
    for n in order:
        part1[n] = first_sum(n, flying[n])
        flying[n] = scatter(1, n, part1.at[n], land2)
    for n in order:
        part2[n] = reduce(1, n, part1.at[n], land2, flying[n])
        flying[n] = scatter(2, n, part2.at[n], land3)
    done = {n: reduce(2, n, part2.at[n], land3, flying[n]) for n in order}
    row = None
    for n in range(pieces - 1):
        value = done[n] / total
        cov[:, LANES * n : LANES * (n + 1)] = value
        row = value if row is None else row + value
    variance = done[pieces - 1] / total
    con[...] = row.sum(axis=1, keepdims=True) / jnp.sqrt(variance)
    for copy in started:
        copy.wait_send()


def exchange(operands, owner, cap, total, collective, fused):
    books = owner.shape[0]
    f32 = jnp.float32
    pieces = books // LANES + 1
    rows = books // 128
    dma = pltpu.SemaphoreType.DMA
    out_shape = [
        jax.ShapeDtypeStruct((rows, books), f32),
        jax.ShapeDtypeStruct((rows, LANES), f32),
    ]
    vmem = pl.BlockSpec(memory_space=pltpu.VMEM)
    hbm = pl.BlockSpec(memory_space=pl.ANY)
    if fused:
        sizes, losses = operands
        operands = (sizes.reshape(books // LANES, LANES), owner, losses)
        in_specs = [vmem, hbm, hbm]
        out_shape.append(jax.ShapeDtypeStruct((1, LANES), jnp.int32))
        places = losses.shape[1]
        parts = places // 2048
        scratch = [
            pltpu.VMEM(losses.shape, losses.dtype),
            pltpu.VMEM((books + 2 * LANES, LANES), jnp.int32),
            pltpu.VMEM((WINDOW, places), losses.dtype),
            pltpu.VMEM((4, parts, WINDOW + 2 * PAD, LANES), f32),
            pltpu.VMEM((4, cap, LANES), f32),
            dma((4,)),
        ]
    else:
        facts, xc = operands
        operands = (facts, owner, xc)
        in_specs = [pl.BlockSpec(memory_space=pltpu.SMEM), hbm, vmem]
        scratch = []
    return pl.pallas_call(
        functools.partial(exchange_body, cap, total, fused),
        out_shape=out_shape,
        in_specs=in_specs,
        out_specs=[vmem] * len(out_shape),
        scratch_shapes=scratch + [
            pltpu.SMEM(owner.shape, jnp.int32),
            pltpu.VMEM((3, cap, LANES), f32),
            pltpu.VMEM((2, 1, cap), f32),
            pltpu.VMEM((15, 1, cap), f32),
            pltpu.VMEM((8, 1, cap), f32),
            pltpu.VMEM((4, cap + 2 * PAD, LANES), f32),
            pltpu.VMEM((4, cap + 2 * PAD, LANES), f32),
            pltpu.VMEM((books, LANES), f32),
            pltpu.VMEM((books, LANES), f32),
            pltpu.VMEM((books, LANES), f32),
            pltpu.VMEM((3, books // 2, LANES), f32),
            pltpu.VMEM((pieces, 4, 4, 4, 8, LANES), f32),
            pltpu.VMEM((pieces, 2, 2, 4, 8, LANES), f32),
            pltpu.VMEM((pieces, 2, 4, 4, 8, LANES), f32),
            pltpu.VMEM((pieces, 3, 4, 8, LANES), f32),
            pltpu.VMEM((pieces, 3, 8, LANES), f32),
            pltpu.VMEM((pieces, 4, 4, 8, LANES), f32),
            pltpu.VMEM((pieces, 4, 8, LANES), f32),
            dma((3,)), dma((3,)), dma((22,)), dma((22,)), dma, dma,
            dma((pieces, 6)), dma((pieces, 6)), dma((2, pieces, 3)), dma((2, pieces, 3)), dma,
        ],
        name="exchange_%d" % cap,
        compiler_params=pltpu.CompilerParams(
            collective_id=collective, has_side_effects=True, vmem_limit_bytes=56 << 20
        ),
    )(*operands)


def per_device(losses, book_sizes, owner_books):
    rows, places = losses.shape
    books = book_sizes.shape[0]
    total = rows * lax.axis_size(SCEN)
    cov, con, spare = exchange((book_sizes, losses), owner_books, SHORT, total, 1, True)

    def general(cov, con, losses, sizes, owner):
        xc, facts = segment_sums(losses, sizes)
        return tuple(exchange((facts, xc), owner, books, total, 2, False))

    cov, con = lax.cond(
        spare[0, 0] >= 0,
        lambda cov, con, *rest: (cov, con),
        general,
        cov, con, losses, book_sizes, owner_books,
    )
    return cov, con[:, 0]


def solution(mesh):
    grid = Mesh(mesh.devices.reshape(4, 4, 2, mesh.shape["pos"]), SCEN_POS)
    return jax.shard_map(
        per_device,
        mesh=grid,
        in_specs=(P(SCEN, Y), P(), P()),
        out_specs=(P(SCEN_POS, None), P(SCEN_POS)),
        check_vma=False,
    )
```

```python
import functools

import jax
import jax.numpy as jnp
from jax import lax
from jax.experimental import pallas as pl
from jax.experimental.pallas import tpu as pltpu
from jax.sharding import Mesh
from jax.sharding import PartitionSpec as P

LANES = 128
TILE = 256
SHORT = 384
WINDOW = 128
PAD = 32
GROUPS = ((0, 1), (1, 3), (3, 4))
X, Z, C, Y = "scen_0", "scen_1", "scen_2", "pos"
SCEN = (X, Z, C)
SCEN_POS = (X, Z, C, Y)
COLOURS = (((X, 0), (Z, 0), (Y, 0)), ((Z, 1), (Y, 1), (X, 0)), ((Y, 2), (X, 0), (Z, 0)))


def to_column(row):
    return jnp.broadcast_to(row, (LANES, LANES)).T


def fill_starts(sizes_ref, col, books):
    f32 = jnp.float32
    sizes = sizes_ref[...].astype(f32)
    down = lax.broadcasted_iota(jnp.int32, (LANES, LANES), 0)
    across = lax.broadcasted_iota(jnp.int32, (LANES, LANES), 1)
    upper = jnp.where(down <= across, 1.0, 0.0).astype(f32)
    within = jnp.dot(sizes, upper, precision=lax.Precision.HIGHEST, preferred_element_type=f32)
    before = [jnp.zeros((1, LANES), f32)]
    for k in range(books // LANES - 1):
        before.append(before[-1] + within[k : k + 1, LANES - 1 : LANES])
    start = within - sizes + jnp.concatenate(before, axis=0)
    for k in range(books // LANES):
        col[LANES * k : LANES * (k + 1), :] = to_column(start[k : k + 1, :]).astype(jnp.int32)
    col[books:, :] = jnp.full((col.shape[0] - books, LANES), 1 << 24, jnp.int32)


def books_at(col, books, place):
    count = jnp.zeros((8, LANES), jnp.int32)
    for b in range(0, books, 8):
        count = count + jnp.where(col[b : b + 8, :] <= place, 1, 0)
    return jnp.sum(count, axis=0, keepdims=True) - 1


def segsum_body(blocks, sizes_ref, x_hbm, out_ref, facts_ref, kept, col, sems):
    books = out_ref.shape[1]
    places = x_hbm.shape[1]
    me = lax.axis_index(Y)
    f32 = jnp.float32
    copies = []
    for n, (at, width) in enumerate(blocks):
        piece = pl.ds(at, width)
        copies.append(pltpu.make_async_copy(x_hbm.at[:, piece], kept.at[:, piece], sems.at[n]))
        copies[-1].start()

    fill_starts(sizes_ref, col, books)

    lane = lax.broadcasted_iota(jnp.int32, (1, LANES), 1)
    place = jnp.zeros((1, LANES), jnp.int32)
    for n, (at, width) in enumerate(blocks):
        place = jnp.where(lane == n, me * places + at, place)
        place = jnp.where(lane == 16 + n, me * places + at + width - 1, place)
    for j in range(4):
        place = jnp.where(lane == 32 + j, j * places, place)
        place = jnp.where(lane == 48 + j, j * places + places - 1, place)
    facts = books_at(col, books, place)
    facts = jnp.where((lane >= 32) & (lane < 48), facts // 8 * 8, facts)

    def fact(i):
        return jnp.sum(jnp.where(lane == i, facts, 0))

    facts_ref[...] = facts
    mine = fact(32 + me)
    spans = [((fact(n) - mine) // TILE, (fact(16 + n) - mine) // TILE) for n in range(len(blocks))]
    out_ref[...] = jnp.zeros_like(out_ref)

    lanes = lax.broadcasted_iota(jnp.int32, (TILE, LANES), 1)
    for n, (at, width) in enumerate(blocks):
        base = me * places + at
        copies[n].wait()

        def add_tile(t, carry):
            r0 = pl.multiple_of(t * TILE, TILE)
            g0 = pl.multiple_of(mine + r0, 8)
            begin = col[pl.ds(g0, TILE), :] - base
            end = col[pl.ds(g0 + 1, TILE), :] - base
            parts = []
            for l in range(0, width, LANES):
                inside = (lanes + l >= begin) & (lanes + l < end)
                parts.append(jnp.where(inside, 1.0, 0.0).astype(jnp.bfloat16))
            sums = lax.dot_general(
                jnp.concatenate(parts, axis=1), kept[:, at : at + width],
                (((1,), (1,)), ((), ())), preferred_element_type=f32,
            )
            for c in range(out_ref.shape[0]):
                out_ref[c, pl.ds(r0, TILE), :] += sums[:, LANES * c : LANES * (c + 1)]
            return carry

        lax.fori_loop(spans[n][0], spans[n][1] + 1, add_tile, 0)


def segment_sums(losses, sizes):
    rows, places = losses.shape
    books = sizes.shape[0]
    widths = [places // 4] * 3 + [places // 8] * 2
    blocks = tuple((sum(widths[:n]), w) for n, w in enumerate(widths))
    return pl.pallas_call(
        functools.partial(segsum_body, blocks),
        out_shape=(
            jax.ShapeDtypeStruct((rows // LANES, books, LANES), jnp.float32),
            jax.ShapeDtypeStruct((1, LANES), jnp.int32),
        ),
        in_specs=[pl.BlockSpec(memory_space=pltpu.VMEM), pl.BlockSpec(memory_space=pl.ANY)],
        out_specs=[pl.BlockSpec(memory_space=pltpu.VMEM)] * 2,
        scratch_shapes=[
            pltpu.VMEM((rows, places), jnp.bfloat16),
            pltpu.VMEM((2 * books + TILE, LANES), jnp.int32),
            pltpu.SemaphoreType.DMA((len(blocks),)),
        ],
        name="segment_sums",
        compiler_params=pltpu.CompilerParams(vmem_limit_bytes=48 << 20),
    )(sizes.reshape(books // LANES, LANES), losses)


def split(x):
    high = x.astype(jnp.bfloat16)
    return high, (x - high.astype(jnp.float32)).astype(jnp.bfloat16)


def exchange_body(cap, total, fused, *refs):
    if fused:
        sizes, owners, x_hbm, cov, con, facts_ref = refs[:6]
        kept, col, masks, sums_at, xc, csem = refs[6:12]
        refs = refs[12:]
    else:
        offs, owners, xc, cov, con = refs[:5]
        refs = refs[5:]
    (
        owner, land, vsum, xvec, yvec, z, zmean, full0, full1, mean, own, gram, relay, land1, land2, land3,
        part1, part2, ysend, yrecv, vsend, vrecv, psend, precv, esend, erecv, rsend, rrecv, osem,
    ) = refs
    at = {name: lax.axis_index(name) for name in SCEN_POS}
    size = {X: 4, Z: 4, C: 2, Y: 4}
    full = (full0, full1)
    books = full0.shape[0]

    def peer(name, p):
        return lax.rem(at[name] + p, size[name])

    fetch = pltpu.make_async_copy(owners, owner, osem)
    fetch.start()
    around = [(a, b) for a in range(size[X]) for b in range(size[Z]) if a or b]
    along = [(d, p) for p in (2, 1, 3, 0) for d in range(size[C]) if d or p]
    others = [{X: peer(X, a), Z: peer(Z, b)} for a, b in around]
    others += [{C: peer(C, d), Y: peer(Y, p)} for d, p in along]
    if fused:
        loads = []
        for n, p in enumerate((2, 1, 3, 0)):
            rows = pl.ds(pl.multiple_of(peer(Y, p) * LANES, LANES), LANES)
            loads.append(
                pltpu.make_async_copy(
                    x_hbm.at[rows, :], kept.at[pl.ds(LANES * n, LANES), :], csem.at[n]
                )
            )
            loads[-1].start()
    barrier = pltpu.get_barrier_semaphore()
    for other in others:
        pl.semaphore_signal(barrier, inc=1, device_id=other, device_id_type=pl.DeviceIdType.MESH)
    if not fused:
        pl.semaphore_wait(barrier, len(others))

    def send_to(src, dst, s, r, device):
        copy = pltpu.make_async_remote_copy(
            src_ref=src,
            dst_ref=dst,
            send_sem=s,
            recv_sem=r,
            device_id=device,
            device_id_type=pl.DeviceIdType.MESH,
        )
        copy.start()
        return copy

    def send(src, dst, s, r, name, p):
        return send_to(src, dst, s, r, {name: peer(name, p)})

    started = []
    zero = jnp.zeros((PAD, LANES), jnp.float32)
    chunks = []

    def send_chunk(slot):
        p = (2, 1, 3)[slot]
        source = xc.at[slot] if fused else xc.at[peer(Y, p), pl.ds(0, cap), :]
        chunks.append(send(source, land.at[p - 1], ysend.at[p - 1], yrecv.at[p - 1], Y, p))

    if fused:
        places = x_hbm.shape[1]
        width = masks.shape[1] // sums_at.shape[1]
        parts = places // width
        fill_starts(sizes, col, books)
        lane = lax.broadcasted_iota(jnp.int32, (1, LANES), 1)
        blocks = 4 * parts
        step = jnp.where(lane < blocks, width, places)
        place = jnp.where(lane < blocks, lane, lane - blocks) * step
        early = books_at(col, books, place) // 8 * 8
        span = books_at(col, books, place + step - 1) - early
        spare = jnp.where(
            lane < blocks, WINDOW - 1 - span, jnp.where(lane < blocks + 4, cap - 1 - span, 0)
        )
        facts_ref[...] = jnp.broadcast_to(jnp.min(spare, axis=1, keepdims=True), (1, LANES))

        def fact(i):
            return jnp.sum(jnp.where(lane == i, early, 0))

        first = [fact(blocks + lax.rem(at[Y] + 4 - p, 4)) for p in range(4)]
        begins = [fact(at[Y] * parts + i) for i in range(parts)]
        lanes = lax.broadcasted_iota(jnp.int32, (WINDOW, LANES), 1)

        def member(i):
            base = at[Y] * places + i * width
            low = col[pl.ds(begins[i], WINDOW), :] - base
            high = col[pl.ds(begins[i] + 1, WINDOW), :] - base
            tiles = []
            for l in range(0, width, LANES):
                inside = (lanes + l >= low) & (lanes + l < high)
                tiles.append(jnp.where(inside, 1.0, 0.0).astype(jnp.bfloat16))
            return jnp.concatenate(tiles, axis=1)

        for i in range(parts):
            for q in range(4):
                sums_at[q, i, 0:PAD, :] = zero
                sums_at[q, i, PAD + WINDOW :, :] = zero
        for a, b in GROUPS:
            for q in range(a, b):
                loads[q].wait()
            for i in range(parts):
                piece = slice(i * width, (i + 1) * width)
                if a == 0:
                    chosen = member(i)
                    masks[:, piece] = chosen
                else:
                    chosen = masks[:, piece]
                got = lax.dot_general(
                    chosen, kept[LANES * a : LANES * b, piece],
                    (((1,), (1,)), ((), ())), preferred_element_type=jnp.float32,
                )
                for q in range(a, b):
                    sums_at[q, i, PAD : PAD + WINDOW, :] = got[:, LANES * (q - a) : LANES * (q - a + 1)]

            def combine(t, carry):
                for q in range(a, b):
                    value = None
                    for i in range(parts):
                        u = lax.min(lax.max(t * PAD - (begins[i] - first[0]) + PAD, 0), WINDOW + PAD)
                        got = sums_at[q, i, pl.ds(u, PAD), :]
                        value = got if value is None else value + got
                    xc[q, pl.ds(pl.multiple_of(t * PAD, PAD), PAD), :] = value
                return carry

            lax.fori_loop(0, cap // PAD, combine, 0, unroll=2)
            if a == 0:
                pl.semaphore_wait(barrier, len(others))
            for q in range(a, min(b, 3)):
                send_chunk(q)
    else:
        first = [offs[0, 32 + lax.rem(at[Y] + 4 - p, 4)] for p in range(4)]
        for q in range(3):
            send_chunk(q)

    for b in range(0, cap, LANES):
        rows = slice(b, b + LANES)
        block = (xc[0, rows, :] + xc[1, rows, :]) + (xc[2, rows, :] + xc[3, rows, :])
        vsum[0, :, rows] = block.T.sum(axis=0, keepdims=True)
    xcopies = []
    for n, (a, b) in enumerate(around):
        xcopies.append(
            send_to(vsum.at[0], xvec.at[n], vsend.at[n], vrecv.at[n], {X: peer(X, a), Z: peer(Z, b)})
        )
    value = vsum[0]
    for n, copy in enumerate(xcopies):
        copy.wait_recv()
        value = value + xvec[n]
    vsum[1] = value
    started += xcopies
    ycopies = {}
    for n, (d, p) in enumerate(along):
        slot = len(around) + n
        ycopies[d, p] = send_to(
            vsum.at[1], yvec.at[4 * d + p], vsend.at[slot], vrecv.at[slot],
            {C: peer(C, d), Y: peer(Y, p)},
        )
    started += ycopies.values()


    for p in range(4):
        for ref in (z, zmean):
            ref[p, 0:PAD, :] = zero
            ref[p, cap + PAD :, :] = zero
    z[0, PAD : PAD + cap, :] = xc[3] if fused else xc[at[Y], 0:cap, :]
    for copy, p in zip(chunks, (2, 1, 3)):
        copy.wait_recv()
        z[p, PAD : PAD + cap, :] = land[p - 1]
    started += chunks

    def place_books(source, target):
        def put(t, carry):
            row = t * PAD
            value = None
            for p in range(4):
                u = lax.min(lax.max(row - first[p] + PAD, 0), cap + PAD)
                got = source[p, pl.ds(u, PAD), :]
                value = got if value is None else value + got
            target[pl.ds(pl.multiple_of(row, PAD), PAD), :] = value
            return carry

        lax.fori_loop(0, books // PAD, put, 0, unroll=2)

    place_books(z, full0)
    pair = send(full0, full1, psend, precv, C, 1)
    started.append(pair)

    core = at[C]

    def gather(source, h):
        def some(g, carry):
            k0 = (g // 4) * 64 + core * 32 + lax.rem(g, 4) * 8
            for r in range(8):
                book = owner[k0 + r]
                own[h, pl.ds(g * 8 + r, 1), :] = source[pl.ds(book, 1), :]
            return carry

        lax.fori_loop(0, own.shape[1] // 8, some, 0, unroll=2)

    fetch.wait()
    gather(full0, 0)

    for p in range(4):
        sums = vsum[1] if p == 0 else None
        for d in (0, 1):
            if d or p:
                ycopies[d, p].wait_recv()
                sums = yvec[4 * d + p] if sums is None else sums + yvec[4 * d + p]
        average = sums / total
        for b in range(0, cap, LANES):
            zmean[p, PAD + b : PAD + b + LANES, :] = to_column(average[:, b : b + LANES])
    place_books(zmean, mean)
    gather(mean, 2)
    pair.wait_recv()
    gather(full1, 1)

    pieces = books // LANES + 1
    each = pieces // 3

    def pick(ref, dim, index):
        return ref.at[(slice(None),) * dim + (index,)]

    def half(n, index, h):
        dim = COLOURS[n // each][0][1]
        some = pl.ds(2 * h, 2)
        where = [(index, some), (some, index), (some, slice(None), index)][dim]
        return gram.at[(n, *where)]

    def first_out(n):
        name = COLOURS[n // each][0][0]
        ahead, behind = peer(name, 1), peer(name, 3)
        copies = []
        for k, (index, h, target, p) in enumerate((
            (peer(name, 2), 0, relay.at[n, 0], 1),
            (peer(name, 2), 1, relay.at[n, 1], 3),
            (ahead, 1, land1.at[n, 0, pl.ds(2, 2)], 1),
            (behind, 0, land1.at[n, 1, pl.ds(0, 2)], 3),
        )):
            copies.append(send(half(n, index, h), target, esend.at[n, k], erecv.at[n, k], name, p))
        return copies

    def first_relay(n, copies):
        name = COLOURS[n // each][0][0]
        for h, p in ((0, 1), (1, 3)):
            copies[h].wait_recv()
            relay[n, h] = relay[n, h] + half(n, peer(name, p), h)[...]
            copies.append(
                send(
                    relay.at[n, h], land1.at[n, h, pl.ds(2 * h, 2)],
                    esend.at[n, 4 + h], erecv.at[n, 4 + h], name, p,
                )
            )

    def first_sum(n, copies):
        name, dim = COLOURS[n // each][0]
        for copy in copies[2:]:
            copy.wait_recv()
        started.extend(copies)
        return pick(gram.at[n], dim, at[name])[...] + (land1[n, 0] + land1[n, 1])

    def scatter(stage, n, source, lands):
        name, dim = COLOURS[n // each][stage]
        copies = []
        for p in (2, 1, 3):
            copies.append(
                (p, send(
                    pick(source, dim, peer(name, p)), lands.at[n, p - 1],
                    rsend.at[stage - 1, n, p - 1], rrecv.at[stage - 1, n, p - 1], name, p,
                ))
            )
        return copies

    def reduce(stage, n, source, lands, copies):
        name, dim = COLOURS[n // each][stage]
        value = pick(source, dim, at[name])[...]
        for p, copy in copies:
            copy.wait_recv()
            value = value + lands[n, p - 1]
            started.append(copy)
        return value

    order = [each * c + q for q in range(each) for c in range(3)]
    flying = {}
    a0h, a0l = split(own[0] - own[2])
    a1h, a1l = split(own[1] - own[2])
    left = jnp.concatenate([a0h, a1h, a0h, a1h, a0l, a1l], axis=1)
    for k in range(0, pieces, 2):
        pair = order[k : k + 2]
        if k < pieces - 1:
            right = []
            for n in pair:
                rows = slice(LANES * n, LANES * (n + 1))
                b0h, b0l = split(full0[rows, :] - mean[rows, :])
                b1h, b1l = split(full1[rows, :] - mean[rows, :])
                right.append(jnp.concatenate([b0h, b1h, b0l, b1l, b0h, b1h], axis=1))
            got = lax.dot_general(
                left, jnp.concatenate(right, axis=0), (((1,), (1,)), ((), ())),
                preferred_element_type=jnp.float32,
            )
            for m, n in enumerate(pair):
                gram[n] = got[:, LANES * m : LANES * (m + 1)].reshape(4, 4, 4, 8, LANES)
        else:
            square = None
            for ref in (full0, full1):
                whole = (ref[...] - mean[...]).reshape(books // 8, 8, LANES).sum(axis=0)
                whole = whole.sum(axis=0, keepdims=True)
                square = whole * whole if square is None else square + whole * whole
            square = square.sum(axis=1, keepdims=True)
            gram[pieces - 1] = jnp.broadcast_to(square, (4, 4, 4, 8, LANES))
        for n in pair:
            flying[n] = first_out(n)
    for n in order:
        first_relay(n, flying[n])
    for n in order:
        part1[n] = first_sum(n, flying[n])
        flying[n] = scatter(1, n, part1.at[n], land2)
    for n in order:
        part2[n] = reduce(1, n, part1.at[n], land2, flying[n])
        flying[n] = scatter(2, n, part2.at[n], land3)
    done = {n: reduce(2, n, part2.at[n], land3, flying[n]) for n in order}
    row = None
    for n in range(pieces - 1):
        value = done[n] / total
        cov[:, LANES * n : LANES * (n + 1)] = value
        row = value if row is None else row + value
    variance = done[pieces - 1] / total
    con[...] = row.sum(axis=1, keepdims=True) / jnp.sqrt(variance)
    for copy in started:
        copy.wait_send()


def exchange(operands, owner, cap, total, collective, fused):
    books = owner.shape[0]
    f32 = jnp.float32
    pieces = books // LANES + 1
    rows = books // 128
    dma = pltpu.SemaphoreType.DMA
    out_shape = [
        jax.ShapeDtypeStruct((rows, books), f32),
        jax.ShapeDtypeStruct((rows, LANES), f32),
    ]
    vmem = pl.BlockSpec(memory_space=pltpu.VMEM)
    hbm = pl.BlockSpec(memory_space=pl.ANY)
    if fused:
        sizes, losses = operands
        operands = (sizes.reshape(books // LANES, LANES), owner, losses)
        in_specs = [vmem, hbm, hbm]
        out_shape.append(jax.ShapeDtypeStruct((1, LANES), jnp.int32))
        places = losses.shape[1]
        parts = places // 2048
        scratch = [
            pltpu.VMEM(losses.shape, losses.dtype),
            pltpu.VMEM((books + 2 * LANES, LANES), jnp.int32),
            pltpu.VMEM((WINDOW, places), losses.dtype),
            pltpu.VMEM((4, parts, WINDOW + 2 * PAD, LANES), f32),
            pltpu.VMEM((4, cap, LANES), f32),
            dma((4,)),
        ]
    else:
        facts, xc = operands
        operands = (facts, owner, xc)
        in_specs = [pl.BlockSpec(memory_space=pltpu.SMEM), hbm, vmem]
        scratch = []
    return pl.pallas_call(
        functools.partial(exchange_body, cap, total, fused),
        out_shape=out_shape,
        in_specs=in_specs,
        out_specs=[vmem] * len(out_shape),
        scratch_shapes=scratch + [
            pltpu.SMEM(owner.shape, jnp.int32),
            pltpu.VMEM((3, cap, LANES), f32),
            pltpu.VMEM((2, 1, cap), f32),
            pltpu.VMEM((15, 1, cap), f32),
            pltpu.VMEM((8, 1, cap), f32),
            pltpu.VMEM((4, cap + 2 * PAD, LANES), f32),
            pltpu.VMEM((4, cap + 2 * PAD, LANES), f32),
            pltpu.VMEM((books, LANES), f32),
            pltpu.VMEM((books, LANES), f32),
            pltpu.VMEM((books, LANES), f32),
            pltpu.VMEM((3, books // 2, LANES), f32),
            pltpu.VMEM((pieces, 4, 4, 4, 8, LANES), f32),
            pltpu.VMEM((pieces, 2, 2, 4, 8, LANES), f32),
            pltpu.VMEM((pieces, 2, 4, 4, 8, LANES), f32),
            pltpu.VMEM((pieces, 3, 4, 8, LANES), f32),
            pltpu.VMEM((pieces, 3, 8, LANES), f32),
            pltpu.VMEM((pieces, 4, 4, 8, LANES), f32),
            pltpu.VMEM((pieces, 4, 8, LANES), f32),
            dma((3,)), dma((3,)), dma((22,)), dma((22,)), dma, dma,
            dma((pieces, 6)), dma((pieces, 6)), dma((2, pieces, 3)), dma((2, pieces, 3)), dma,
        ],
        name="exchange_%d" % cap,
        compiler_params=pltpu.CompilerParams(
            collective_id=collective, has_side_effects=True, vmem_limit_bytes=56 << 20
        ),
    )(*operands)


def per_device(losses, book_sizes, owner_books):
    rows, places = losses.shape
    books = book_sizes.shape[0]
    total = rows * lax.axis_size(SCEN)
    cov, con, spare = exchange((book_sizes, losses), owner_books, SHORT, total, 1, True)

    def general(cov, con, losses, sizes, owner):
        xc, facts = segment_sums(losses, sizes)
        return tuple(exchange((facts, xc), owner, books, total, 2, False))

    cov, con = lax.cond(
        spare[0, 0] >= 0,
        lambda cov, con, *rest: (cov, con),
        general,
        cov, con, losses, book_sizes, owner_books,
    )
    return cov, con[:, 0]


def solution(mesh):
    grid = Mesh(mesh.devices.reshape(4, 4, 2, mesh.shape["pos"]), SCEN_POS)
    return jax.shard_map(
        per_device,
        mesh=grid,
        in_specs=(P(SCEN, Y), P(), P()),
        out_specs=(P(SCEN_POS, None), P(SCEN_POS)),
        check_vma=False,
    )
```

```python
import functools

import jax
import jax.numpy as jnp
from jax import lax
from jax.experimental import pallas as pl
from jax.experimental.pallas import tpu as pltpu
from jax.sharding import Mesh
from jax.sharding import PartitionSpec as P

LANES = 128
TILE = 256
SHORT = 384
WINDOW = 128
PAD = 32
GROUPS = ((0, 1), (1, 3), (3, 4))
X, Z, C, Y = "scen_0", "scen_1", "scen_2", "pos"
SCEN = (X, Z, C)
SCEN_POS = (X, Z, C, Y)
COLOURS = (((X, 0), (Z, 0), (Y, 0)), ((Z, 1), (Y, 1), (X, 0)), ((Y, 2), (X, 0), (Z, 0)))


def to_column(row):
    return jnp.broadcast_to(row, (LANES, LANES)).T


def fill_starts(sizes_ref, col, books):
    f32 = jnp.float32
    sizes = sizes_ref[...].astype(f32)
    down = lax.broadcasted_iota(jnp.int32, (LANES, LANES), 0)
    across = lax.broadcasted_iota(jnp.int32, (LANES, LANES), 1)
    upper = jnp.where(down <= across, 1.0, 0.0).astype(f32)
    within = jnp.dot(sizes, upper, precision=lax.Precision.HIGHEST, preferred_element_type=f32)
    before = [jnp.zeros((1, LANES), f32)]
    for k in range(books // LANES - 1):
        before.append(before[-1] + within[k : k + 1, LANES - 1 : LANES])
    start = within - sizes + jnp.concatenate(before, axis=0)
    for k in range(books // LANES):
        col[LANES * k : LANES * (k + 1), :] = to_column(start[k : k + 1, :]).astype(jnp.int32)
    col[books:, :] = jnp.full((col.shape[0] - books, LANES), 1 << 24, jnp.int32)


def books_at(col, books, place):
    counts = [jnp.zeros((8, LANES), jnp.int32) for _ in range(8)]
    for b in range(0, books, 8):
        k = b // 8 % 8
        counts[k] = counts[k] + jnp.where(col[b : b + 8, :] <= place, 1, 0)
    return jnp.sum(sum(counts), axis=0, keepdims=True) - 1


def segsum_body(blocks, sizes_ref, x_hbm, out_ref, facts_ref, kept, col, sems):
    books = out_ref.shape[1]
    places = x_hbm.shape[1]
    me = lax.axis_index(Y)
    f32 = jnp.float32
    copies = []
    for n, (at, width) in enumerate(blocks):
        piece = pl.ds(at, width)
        copies.append(pltpu.make_async_copy(x_hbm.at[:, piece], kept.at[:, piece], sems.at[n]))
        copies[-1].start()

    fill_starts(sizes_ref, col, books)

    lane = lax.broadcasted_iota(jnp.int32, (1, LANES), 1)
    place = jnp.zeros((1, LANES), jnp.int32)
    for n, (at, width) in enumerate(blocks):
        place = jnp.where(lane == n, me * places + at, place)
        place = jnp.where(lane == 16 + n, me * places + at + width - 1, place)
    for j in range(4):
        place = jnp.where(lane == 32 + j, j * places, place)
        place = jnp.where(lane == 48 + j, j * places + places - 1, place)
    facts = books_at(col, books, place)
    facts = jnp.where((lane >= 32) & (lane < 48), facts // 8 * 8, facts)

    def fact(i):
        return jnp.sum(jnp.where(lane == i, facts, 0))

    facts_ref[...] = facts
    mine = fact(32 + me)
    spans = [((fact(n) - mine) // TILE, (fact(16 + n) - mine) // TILE) for n in range(len(blocks))]
    out_ref[...] = jnp.zeros_like(out_ref)

    lanes = lax.broadcasted_iota(jnp.int32, (TILE, LANES), 1)
    for n, (at, width) in enumerate(blocks):
        base = me * places + at
        copies[n].wait()

        def add_tile(t, carry):
            r0 = pl.multiple_of(t * TILE, TILE)
            g0 = pl.multiple_of(mine + r0, 8)
            begin = col[pl.ds(g0, TILE), :] - base
            end = col[pl.ds(g0 + 1, TILE), :] - base
            parts = []
            for l in range(0, width, LANES):
                inside = (lanes + l >= begin) & (lanes + l < end)
                parts.append(jnp.where(inside, 1.0, 0.0).astype(jnp.bfloat16))
            sums = lax.dot_general(
                jnp.concatenate(parts, axis=1), kept[:, at : at + width],
                (((1,), (1,)), ((), ())), preferred_element_type=f32,
            )
            for c in range(out_ref.shape[0]):
                out_ref[c, pl.ds(r0, TILE), :] += sums[:, LANES * c : LANES * (c + 1)]
            return carry

        lax.fori_loop(spans[n][0], spans[n][1] + 1, add_tile, 0)


def segment_sums(losses, sizes):
    rows, places = losses.shape
    books = sizes.shape[0]
    widths = [places // 4] * 3 + [places // 8] * 2
    blocks = tuple((sum(widths[:n]), w) for n, w in enumerate(widths))
    return pl.pallas_call(
        functools.partial(segsum_body, blocks),
        out_shape=(
            jax.ShapeDtypeStruct((rows // LANES, books, LANES), jnp.float32),
            jax.ShapeDtypeStruct((1, LANES), jnp.int32),
        ),
        in_specs=[pl.BlockSpec(memory_space=pltpu.VMEM), pl.BlockSpec(memory_space=pl.ANY)],
        out_specs=[pl.BlockSpec(memory_space=pltpu.VMEM)] * 2,
        scratch_shapes=[
            pltpu.VMEM((rows, places), jnp.bfloat16),
            pltpu.VMEM((2 * books + TILE, LANES), jnp.int32),
            pltpu.SemaphoreType.DMA((len(blocks),)),
        ],
        name="segment_sums",
        compiler_params=pltpu.CompilerParams(vmem_limit_bytes=48 << 20),
    )(sizes.reshape(books // LANES, LANES), losses)


def split(x):
    high = x.astype(jnp.bfloat16)
    return high, (x - high.astype(jnp.float32)).astype(jnp.bfloat16)


def exchange_body(cap, total, fused, *refs):
    if fused:
        sizes, owners, x_hbm, cov, con, facts_ref = refs[:6]
        kept, col, masks, sums_at, xc, csem = refs[6:12]
        refs = refs[12:]
    else:
        offs, owners, xc, cov, con = refs[:5]
        refs = refs[5:]
    (
        owner, land, vsum, xvec, yvec, z, zmean, full0, full1, mean, own, gram, relay, land1, land2, land3,
        part1, part2, ysend, yrecv, vsend, vrecv, psend, precv, esend, erecv, rsend, rrecv, osem,
    ) = refs
    at = {name: lax.axis_index(name) for name in SCEN_POS}
    size = {X: 4, Z: 4, C: 2, Y: 4}
    full = (full0, full1)
    books = full0.shape[0]

    def peer(name, p):
        return lax.rem(at[name] + p, size[name])

    fetch = pltpu.make_async_copy(owners, owner, osem)
    fetch.start()
    around = [(a, b) for a in range(size[X]) for b in range(size[Z]) if a or b]
    along = [(d, p) for p in (2, 1, 3, 0) for d in range(size[C]) if d or p]
    others = [{X: peer(X, a), Z: peer(Z, b)} for a, b in around]
    others += [{C: peer(C, d), Y: peer(Y, p)} for d, p in along]
    if fused:
        loads = []
        for n, p in enumerate((2, 1, 3, 0)):
            rows = pl.ds(pl.multiple_of(peer(Y, p) * LANES, LANES), LANES)
            loads.append(
                pltpu.make_async_copy(
                    x_hbm.at[rows, :], kept.at[pl.ds(LANES * n, LANES), :], csem.at[n]
                )
            )
            loads[-1].start()
    barrier = pltpu.get_barrier_semaphore()
    for other in others:
        pl.semaphore_signal(barrier, inc=1, device_id=other, device_id_type=pl.DeviceIdType.MESH)
    if not fused:
        pl.semaphore_wait(barrier, len(others))

    def send_to(src, dst, s, r, device):
        copy = pltpu.make_async_remote_copy(
            src_ref=src,
            dst_ref=dst,
            send_sem=s,
            recv_sem=r,
            device_id=device,
            device_id_type=pl.DeviceIdType.MESH,
        )
        copy.start()
        return copy

    def send(src, dst, s, r, name, p):
        return send_to(src, dst, s, r, {name: peer(name, p)})

    started = []
    zero = jnp.zeros((PAD, LANES), jnp.float32)
    chunks = []

    def send_chunk(slot):
        p = (2, 1, 3)[slot]
        source = xc.at[slot] if fused else xc.at[peer(Y, p), pl.ds(0, cap), :]
        chunks.append(send(source, land.at[p - 1], ysend.at[p - 1], yrecv.at[p - 1], Y, p))

    if fused:
        places = x_hbm.shape[1]
        width = masks.shape[1] // sums_at.shape[1]
        parts = places // width
        fill_starts(sizes, col, books)
        lane = lax.broadcasted_iota(jnp.int32, (1, LANES), 1)
        blocks = 4 * parts
        step = jnp.where(lane < blocks, width, places)
        place = jnp.where(lane < blocks, lane, lane - blocks) * step
        early = books_at(col, books, place) // 8 * 8
        span = books_at(col, books, place + step - 1) - early
        spare = jnp.where(
            lane < blocks, WINDOW - 1 - span, jnp.where(lane < blocks + 4, cap - 1 - span, 0)
        )
        facts_ref[...] = jnp.broadcast_to(jnp.min(spare, axis=1, keepdims=True), (1, LANES))

        def fact(i):
            return jnp.sum(jnp.where(lane == i, early, 0))

        first = [fact(blocks + lax.rem(at[Y] + 4 - p, 4)) for p in range(4)]
        begins = [fact(at[Y] * parts + i) for i in range(parts)]
        lanes = lax.broadcasted_iota(jnp.int32, (WINDOW, LANES), 1)

        def member(i):
            base = at[Y] * places + i * width
            low = col[pl.ds(begins[i], WINDOW), :] - base
            high = col[pl.ds(begins[i] + 1, WINDOW), :] - base
            tiles = []
            for l in range(0, width, LANES):
                inside = (lanes + l >= low) & (lanes + l < high)
                tiles.append(jnp.where(inside, 1.0, 0.0).astype(jnp.bfloat16))
            return jnp.concatenate(tiles, axis=1)

        for i in range(parts):
            for q in range(4):
                sums_at[q, i, 0:PAD, :] = zero
                sums_at[q, i, PAD + WINDOW :, :] = zero
        for a, b in GROUPS:
            for q in range(a, b):
                loads[q].wait()
            for i in range(parts):
                piece = slice(i * width, (i + 1) * width)
                if a == 0:
                    chosen = member(i)
                    masks[:, piece] = chosen
                else:
                    chosen = masks[:, piece]
                got = lax.dot_general(
                    chosen, kept[LANES * a : LANES * b, piece],
                    (((1,), (1,)), ((), ())), preferred_element_type=jnp.float32,
                )
                for q in range(a, b):
                    sums_at[q, i, PAD : PAD + WINDOW, :] = got[:, LANES * (q - a) : LANES * (q - a + 1)]

            def combine(t, carry):
                for q in range(a, b):
                    value = None
                    for i in range(parts):
                        u = lax.min(lax.max(t * PAD - (begins[i] - first[0]) + PAD, 0), WINDOW + PAD)
                        got = sums_at[q, i, pl.ds(u, PAD), :]
                        value = got if value is None else value + got
                    xc[q, pl.ds(pl.multiple_of(t * PAD, PAD), PAD), :] = value
                return carry

            lax.fori_loop(0, cap // PAD, combine, 0, unroll=4)
            if a == 0:
                pl.semaphore_wait(barrier, len(others))
            for q in range(a, min(b, 3)):
                send_chunk(q)
    else:
        first = [offs[0, 32 + lax.rem(at[Y] + 4 - p, 4)] for p in range(4)]
        for q in range(3):
            send_chunk(q)

    for b in range(0, cap, LANES):
        rows = slice(b, b + LANES)
        block = (xc[0, rows, :] + xc[1, rows, :]) + (xc[2, rows, :] + xc[3, rows, :])
        vsum[0, :, rows] = block.T.sum(axis=0, keepdims=True)
    xcopies = []
    for n, (a, b) in enumerate(around):
        xcopies.append(
            send_to(vsum.at[0], xvec.at[n], vsend.at[n], vrecv.at[n], {X: peer(X, a), Z: peer(Z, b)})
        )
    value = vsum[0]
    for n, copy in enumerate(xcopies):
        copy.wait_recv()
        value = value + xvec[n]
    vsum[1] = value
    started += xcopies
    ycopies = {}
    for n, (d, p) in enumerate(along):
        slot = len(around) + n
        ycopies[d, p] = send_to(
            vsum.at[1], yvec.at[4 * d + p], vsend.at[slot], vrecv.at[slot],
            {C: peer(C, d), Y: peer(Y, p)},
        )
    started += ycopies.values()


    for p in range(4):
        for ref in (z, zmean):
            ref[p, 0:PAD, :] = zero
            ref[p, cap + PAD :, :] = zero
    z[0, PAD : PAD + cap, :] = xc[3] if fused else xc[at[Y], 0:cap, :]
    for copy, p in zip(chunks, (2, 1, 3)):
        copy.wait_recv()
        z[p, PAD : PAD + cap, :] = land[p - 1]
    started += chunks

    def place_books(source, target):
        def put(t, carry):
            row = t * PAD
            value = None
            for p in range(4):
                u = lax.min(lax.max(row - first[p] + PAD, 0), cap + PAD)
                got = source[p, pl.ds(u, PAD), :]
                value = got if value is None else value + got
            target[pl.ds(pl.multiple_of(row, PAD), PAD), :] = value
            return carry

        lax.fori_loop(0, books // PAD, put, 0, unroll=8)

    place_books(z, full0)
    pair = send(full0, full1, psend, precv, C, 1)
    started.append(pair)

    core = at[C]

    def gather(source, h):
        def some(g, carry):
            k0 = (g // 4) * 64 + core * 32 + lax.rem(g, 4) * 8
            for r in range(8):
                book = owner[k0 + r]
                own[h, pl.ds(g * 8 + r, 1), :] = source[pl.ds(book, 1), :]
            return carry

        lax.fori_loop(0, own.shape[1] // 8, some, 0, unroll=8)

    fetch.wait()
    gather(full0, 0)

    for p in range(4):
        sums = vsum[1] if p == 0 else None
        for d in (0, 1):
            if d or p:
                ycopies[d, p].wait_recv()
                sums = yvec[4 * d + p] if sums is None else sums + yvec[4 * d + p]
        average = sums / total
        for b in range(0, cap, LANES):
            zmean[p, PAD + b : PAD + b + LANES, :] = to_column(average[:, b : b + LANES])
    place_books(zmean, mean)
    gather(mean, 2)
    pair.wait_recv()
    gather(full1, 1)

    pieces = books // LANES + 1
    each = pieces // 3

    def pick(ref, dim, index):
        return ref.at[(slice(None),) * dim + (index,)]

    def half(n, index, h):
        dim = COLOURS[n // each][0][1]
        some = pl.ds(2 * h, 2)
        where = [(index, some), (some, index), (some, slice(None), index)][dim]
        return gram.at[(n, *where)]

    def first_out(n):
        name = COLOURS[n // each][0][0]
        ahead, behind = peer(name, 1), peer(name, 3)
        copies = []
        for k, (index, h, target, p) in enumerate((
            (peer(name, 2), 0, relay.at[n, 0], 1),
            (peer(name, 2), 1, relay.at[n, 1], 3),
            (ahead, 1, land1.at[n, 0, pl.ds(2, 2)], 1),
            (behind, 0, land1.at[n, 1, pl.ds(0, 2)], 3),
        )):
            copies.append(send(half(n, index, h), target, esend.at[n, k], erecv.at[n, k], name, p))
        return copies

    def first_relay(n, copies):
        name = COLOURS[n // each][0][0]
        for h, p in ((0, 1), (1, 3)):
            copies[h].wait_recv()
            relay[n, h] = relay[n, h] + half(n, peer(name, p), h)[...]
            copies.append(
                send(
                    relay.at[n, h], land1.at[n, h, pl.ds(2 * h, 2)],
                    esend.at[n, 4 + h], erecv.at[n, 4 + h], name, p,
                )
            )

    def first_sum(n, copies):
        name, dim = COLOURS[n // each][0]
        for copy in copies[2:]:
            copy.wait_recv()
        started.extend(copies)
        return pick(gram.at[n], dim, at[name])[...] + (land1[n, 0] + land1[n, 1])

    def scatter(stage, n, source, lands):
        name, dim = COLOURS[n // each][stage]
        copies = []
        for p in (2, 1, 3):
            copies.append(
                (p, send(
                    pick(source, dim, peer(name, p)), lands.at[n, p - 1],
                    rsend.at[stage - 1, n, p - 1], rrecv.at[stage - 1, n, p - 1], name, p,
                ))
            )
        return copies

    def reduce(stage, n, source, lands, copies):
        name, dim = COLOURS[n // each][stage]
        value = pick(source, dim, at[name])[...]
        for p, copy in copies:
            copy.wait_recv()
            value = value + lands[n, p - 1]
            started.append(copy)
        return value

    order = [each * c + q for q in range(each) for c in range(3)]
    flying = {}
    a0h, a0l = split(own[0] - own[2])
    a1h, a1l = split(own[1] - own[2])
    left = jnp.concatenate([a0h, a1h, a0h, a1h, a0l, a1l], axis=1)
    for k in range(0, pieces, 2):
        pair = order[k : k + 2]
        if k < pieces - 1:
            right = []
            for n in pair:
                rows = slice(LANES * n, LANES * (n + 1))
                b0h, b0l = split(full0[rows, :] - mean[rows, :])
                b1h, b1l = split(full1[rows, :] - mean[rows, :])
                right.append(jnp.concatenate([b0h, b1h, b0l, b1l, b0h, b1h], axis=1))
            got = lax.dot_general(
                left, jnp.concatenate(right, axis=0), (((1,), (1,)), ((), ())),
                preferred_element_type=jnp.float32,
            )
            for m, n in enumerate(pair):
                gram[n] = got[:, LANES * m : LANES * (m + 1)].reshape(4, 4, 4, 8, LANES)
        else:
            square = None
            for ref in (full0, full1):
                whole = (ref[...] - mean[...]).reshape(books // 8, 8, LANES).sum(axis=0)
                whole = whole.sum(axis=0, keepdims=True)
                square = whole * whole if square is None else square + whole * whole
            square = square.sum(axis=1, keepdims=True)
            gram[pieces - 1] = jnp.broadcast_to(square, (4, 4, 4, 8, LANES))
        for n in pair:
            flying[n] = first_out(n)
    for n in order:
        first_relay(n, flying[n])
    for n in order:
        part1[n] = first_sum(n, flying[n])
        flying[n] = scatter(1, n, part1.at[n], land2)
    for n in order:
        part2[n] = reduce(1, n, part1.at[n], land2, flying[n])
        flying[n] = scatter(2, n, part2.at[n], land3)
    done = {n: reduce(2, n, part2.at[n], land3, flying[n]) for n in order}
    row = None
    for n in range(pieces - 1):
        value = done[n] / total
        cov[:, LANES * n : LANES * (n + 1)] = value
        row = value if row is None else row + value
    variance = done[pieces - 1] / total
    con[...] = row.sum(axis=1, keepdims=True) / jnp.sqrt(variance)
    for copy in started:
        copy.wait_send()


def exchange(operands, owner, cap, total, collective, fused):
    books = owner.shape[0]
    f32 = jnp.float32
    pieces = books // LANES + 1
    rows = books // 128
    dma = pltpu.SemaphoreType.DMA
    out_shape = [
        jax.ShapeDtypeStruct((rows, books), f32),
        jax.ShapeDtypeStruct((rows, LANES), f32),
    ]
    vmem = pl.BlockSpec(memory_space=pltpu.VMEM)
    hbm = pl.BlockSpec(memory_space=pl.ANY)
    if fused:
        sizes, losses = operands
        operands = (sizes.reshape(books // LANES, LANES), owner, losses)
        in_specs = [vmem, hbm, hbm]
        out_shape.append(jax.ShapeDtypeStruct((1, LANES), jnp.int32))
        places = losses.shape[1]
        parts = places // 2048
        scratch = [
            pltpu.VMEM(losses.shape, losses.dtype),
            pltpu.VMEM((books + 2 * LANES, LANES), jnp.int32),
            pltpu.VMEM((WINDOW, places), losses.dtype),
            pltpu.VMEM((4, parts, WINDOW + 2 * PAD, LANES), f32),
            pltpu.VMEM((4, cap, LANES), f32),
            dma((4,)),
        ]
    else:
        facts, xc = operands
        operands = (facts, owner, xc)
        in_specs = [pl.BlockSpec(memory_space=pltpu.SMEM), hbm, vmem]
        scratch = []
    return pl.pallas_call(
        functools.partial(exchange_body, cap, total, fused),
        out_shape=out_shape,
        in_specs=in_specs,
        out_specs=[vmem] * len(out_shape),
        scratch_shapes=scratch + [
            pltpu.SMEM(owner.shape, jnp.int32),
            pltpu.VMEM((3, cap, LANES), f32),
            pltpu.VMEM((2, 1, cap), f32),
            pltpu.VMEM((15, 1, cap), f32),
            pltpu.VMEM((8, 1, cap), f32),
            pltpu.VMEM((4, cap + 2 * PAD, LANES), f32),
            pltpu.VMEM((4, cap + 2 * PAD, LANES), f32),
            pltpu.VMEM((books, LANES), f32),
            pltpu.VMEM((books, LANES), f32),
            pltpu.VMEM((books, LANES), f32),
            pltpu.VMEM((3, books // 2, LANES), f32),
            pltpu.VMEM((pieces, 4, 4, 4, 8, LANES), f32),
            pltpu.VMEM((pieces, 2, 2, 4, 8, LANES), f32),
            pltpu.VMEM((pieces, 2, 4, 4, 8, LANES), f32),
            pltpu.VMEM((pieces, 3, 4, 8, LANES), f32),
            pltpu.VMEM((pieces, 3, 8, LANES), f32),
            pltpu.VMEM((pieces, 4, 4, 8, LANES), f32),
            pltpu.VMEM((pieces, 4, 8, LANES), f32),
            dma((3,)), dma((3,)), dma((22,)), dma((22,)), dma, dma,
            dma((pieces, 6)), dma((pieces, 6)), dma((2, pieces, 3)), dma((2, pieces, 3)), dma,
        ],
        name="exchange_%d" % cap,
        compiler_params=pltpu.CompilerParams(
            collective_id=collective, has_side_effects=True, vmem_limit_bytes=56 << 20
        ),
    )(*operands)


def per_device(losses, book_sizes, owner_books):
    rows, places = losses.shape
    books = book_sizes.shape[0]
    total = rows * lax.axis_size(SCEN)
    cov, con, spare = exchange((book_sizes, losses), owner_books, SHORT, total, 1, True)

    def general(cov, con, losses, sizes, owner):
        xc, facts = segment_sums(losses, sizes)
        return tuple(exchange((facts, xc), owner, books, total, 2, False))

    cov, con = lax.cond(
        spare[0, 0] >= 0,
        lambda cov, con, *rest: (cov, con),
        general,
        cov, con, losses, book_sizes, owner_books,
    )
    return cov, con[:, 0]


def solution(mesh):
    grid = Mesh(mesh.devices.reshape(4, 4, 2, mesh.shape["pos"]), SCEN_POS)
    return jax.shard_map(
        per_device,
        mesh=grid,
        in_specs=(P(SCEN, Y), P(), P()),
        out_specs=(P(SCEN_POS, None), P(SCEN_POS)),
        check_vma=False,
    )
```
